256 devices in a mesh: gx: 32 (over z_hi, x, y), gy: 8 (over z_lo, core).
Axes of the slice: x: 4, y: 4, z: 8 (z_hi: 2, z_lo: 4; z = z_hi * 4 + z_lo), core: 2. Of those that a mesh axis runs over, the one named last changes fastest.
Arguments:
- stress: float32 [6, 16, 2048, 1024], P(None, None, 'gx', 'gy'), may hold values from -6 to 6
- velocity: float32 [3, 16, 2048, 1024], P(None, None, 'gx', 'gy'), may hold values from -6 to 6
- material: int32 [16, 2048, 1024], P(None, 'gx', 'gy'), may hold values from 0 to 2
- layer_kind: int32 [16], replicated, may hold values from 0 to 2
- buoyancy: float32 [3], replicated, may hold values from 0.05 to 0.3
- lame_first: float32 [3], replicated, may hold values from 0.05 to 0.3
- shear_modulus: float32 [3], replicated, may hold values from 0.05 to 0.2
- piezo: float32 [3], replicated, may hold values from 0.5 to 2
- permit_lateral: float32 [3], replicated, may hold values from 0.5 to 4
- permit_normal: float32 [3], replicated, may hold values from 0.5 to 4
Outputs:
- stress_next: float32 [6, 16, 2048, 1024], P(None, None, 'gx', 'gy')
- velocity_next: float32 [3, 16, 2048, 1024], P(None, None, 'gx', 'gy')
- potential_modes: float32 [2, 16, 1024, 2048], P(None, None, ('gx', 'gy'))
The draws below stay inside these ranges and needn't reach their ends.
Inputs may be any that keep to these rules, and one draw needn't show every extreme that they name: `layer_kind`: material codes of the layers, as for cells.
All inputs are finite; a program needn't handle non-finite values.
Results may differ from the reference program's by a relative error of at most 0.000076.
Values sent between devices are 32-bit elements; how exact they have to be, the bound alone decides.
No kernel may reach another device: no remote copies, remote signals or barrier semaphores. Data moves between devices by JAX's collectives and lax.ppermute only.
A program may use at most 192 MiB of HBM per device.

```python
import math
import jax
import jax.numpy as jnp

NZ = 16
NX = 2048
NY = 1024


def plant(values, rng, low, high):
    longest = values.shape.index(max(values.shape))
    spots = []
    for shift in (0, 1):
        where = [jax.random.randint(jax.random.fold_in(rng, axis), (), 0, length) for axis, length in enumerate(values.shape)]
        where[longest] = (where[longest] + shift) % values.shape[longest]
        spots.append(tuple(where))
    return values.at[spots[0]].set(low).at[spots[1]].set(high)


def block_levels(key, extent, cuts, low, high):
    gain, own = 1.0, jax.random.fold_in(key, 6)
    for position, blocks in cuts:
        heights = jnp.exp(jax.random.uniform(jax.random.fold_in(own, position), (blocks,), jnp.float32, low / len(cuts), high / len(cuts)))
        gain = gain * jnp.repeat(heights, extent[position] // blocks).reshape([-1 if axis == position else 1 for axis in range(len(extent))])
    return gain


def noise(key, extent, scale, bound, shards=(), kind=jnp.bfloat16):
    entries = scale * jax.random.normal(key, extent, jnp.float32)
    if shards:
        entries = entries * block_levels(key, extent, shards, -0.22, 0.18)
    return jnp.clip(entries, -bound, bound).astype(kind)


def setup_inputs(seed: int = 0) -> dict:
    streams_of = jax.random.split(jax.random.key(seed), 11)
    stress = noise(streams_of[0], (6, NZ, NX, NY), 1.0, 6.0, ((2, 32), (3, 8)), jnp.float32)
    velocity = noise(streams_of[1], (3, NZ, NX, NY), 1.0, 6.0, ((2, 32), (3, 8)), jnp.float32)
    material = plant(jax.random.randint(streams_of[2], (NZ, NX, NY), 0, 3), jax.random.fold_in(streams_of[2], 1), 0, 2).astype(jnp.int32)
    layer_kind = plant(jax.random.randint(streams_of[3], (NZ,), 0, 3), jax.random.fold_in(streams_of[3], 1), 0, 2).astype(jnp.int32)
    buoyancy = jnp.clip(jnp.exp(jax.random.uniform(streams_of[4], (3,), jnp.float32, math.log(0.05), math.log(0.3))), 0.05, 0.3)
    lame_first = jnp.clip(jnp.exp(jax.random.uniform(streams_of[5], (3,), jnp.float32, math.log(0.05), math.log(0.3))), 0.05, 0.3)
    shear_modulus = jnp.clip(jnp.exp(jax.random.uniform(streams_of[6], (3,), jnp.float32, math.log(0.05), math.log(0.2))), 0.05, 0.2)
    piezo = jnp.clip(jnp.exp(jax.random.uniform(streams_of[7], (3,), jnp.float32, math.log(0.5), math.log(2.0))), 0.5, 2.0)
    permit_lateral = jnp.clip(jnp.exp(jax.random.uniform(streams_of[8], (3,), jnp.float32, math.log(0.5), math.log(4.0))), 0.5, 4.0)
    permit_normal = jnp.clip(jnp.exp(jax.random.uniform(streams_of[9], (3,), jnp.float32, math.log(0.5), math.log(4.0))), 0.5, 4.0)
    return {"stress": stress, "velocity": velocity, "material": material, "layer_kind": layer_kind, "buoyancy": buoyancy, "lame_first": lame_first, "shear_modulus": shear_modulus, "piezo": piezo, "permit_lateral": permit_lateral, "permit_normal": permit_normal}


def lookup(codes, table):
    result = jnp.zeros(codes.shape, jnp.float32)
    for material_no in range(3):
        result = result + jnp.where(codes == material_no, table[material_no], 0.0)
    return result


def centre(padded):
    return padded[..., 1:-1, 1:-1]


def x_plus(padded):
    return padded[..., 2:, 1:-1] - padded[..., 1:-1, 1:-1]


def x_minus(padded):
    return padded[..., 1:-1, 1:-1] - padded[..., :-2, 1:-1]


def y_plus(padded):
    return padded[..., 1:-1, 2:] - padded[..., 1:-1, 1:-1]


def y_minus(padded):
    return padded[..., 1:-1, 1:-1] - padded[..., 1:-1, :-2]


def z_plus(inner):
    upper = jnp.concatenate([inner[1:], jnp.zeros_like(inner[:1])], axis=0)
    return upper - inner


def z_minus(inner):
    lower = jnp.concatenate([jnp.zeros_like(inner[:1]), inner[:-1]], axis=0)
    return inner - lower


def advance_velocity(stress_pad, veloc, buoy_field):
    new_x = veloc[0] + buoy_field * (x_plus(stress_pad[0]) + y_minus(stress_pad[3]) + z_minus(centre(stress_pad[4])))
    new_y = veloc[1] + buoy_field * (x_minus(stress_pad[3]) + y_plus(stress_pad[1]) + z_minus(centre(stress_pad[5])))
    new_z = veloc[2] + buoy_field * (x_minus(stress_pad[4]) + y_minus(stress_pad[5]) + z_plus(centre(stress_pad[2])))
    return jnp.stack([new_x, new_y, new_z])


def advance_stress(stress, veloc_pad, lame_field, shear_field):
    strain_x = x_minus(veloc_pad[0])
    strain_y = y_minus(veloc_pad[1])
    strain_z = z_minus(centre(veloc_pad[2]))
    diverge = strain_x + strain_y + strain_z
    new_xx = stress[0] + lame_field * diverge + 2.0 * shear_field * strain_x
    new_yy = stress[1] + lame_field * diverge + 2.0 * shear_field * strain_y
    new_zz = stress[2] + lame_field * diverge + 2.0 * shear_field * strain_z
    new_xy = stress[3] + shear_field * (y_plus(veloc_pad[0]) + x_plus(veloc_pad[1]))
    new_xz = stress[4] + shear_field * (z_plus(centre(veloc_pad[0])) + x_plus(veloc_pad[2]))
    new_yz = stress[5] + shear_field * (z_plus(centre(veloc_pad[1])) + y_plus(veloc_pad[2]))
    return jnp.stack([new_xx, new_yy, new_zz, new_xy, new_xz, new_yz])


def couplings(layer_kind, permit_lateral, permit_normal):
    lateral = lookup(layer_kind, permit_lateral)
    normal = lookup(layer_kind, permit_normal)
    couple = jnp.concatenate([normal[:1], 0.5 * (normal[:-1] + normal[1:]), normal[-1:]])
    return lateral, couple


def solve_layers(rhs, wave, lateral, couple):
    layers = rhs.shape[1]
    factors = []
    carries = []
    for layer_no in range(layers):
        pivot = couple[layer_no] + couple[layer_no + 1] + wave * lateral[layer_no]
        if layer_no > 0:
            pivot = pivot - couple[layer_no] * factors[-1]
            carry = (rhs[:, layer_no] + couple[layer_no] * carries[-1]) / pivot
        else:
            carry = rhs[:, layer_no] / pivot
        factors.append(couple[layer_no + 1] / pivot)
        carries.append(carry)
    solved = [carries[-1]]
    for layer_no in range(layers - 2, -1, -1):
        solved.append(carries[layer_no] + factors[layer_no] * solved[-1])
    return jnp.stack(solved[::-1], axis=1)


def pad_xy(array):
    widths = [(0, 0)] * (array.ndim - 2) + [(1, 1), (1, 1)]
    return jnp.pad(array, widths)


def reference(stress, velocity, material, layer_kind, buoyancy, lame_first, shear_modulus, piezo, permit_lateral, permit_normal):
    buoy_field = lookup(material, buoyancy)
    lame_field = lookup(material, lame_first)
    shear_field = lookup(material, shear_modulus)
    velocity_next = advance_velocity(pad_xy(stress), velocity, buoy_field)
    stress_next = advance_stress(stress, pad_xy(velocity_next), lame_field, shear_field)
    charge = lookup(material, piezo) * (stress_next[4] + stress_next[5])
    spectrum = jnp.fft.fft2(charge, axes=(1, 2), norm="ortho")
    rhs = jnp.stack([jnp.real(spectrum), jnp.imag(spectrum)]).astype(jnp.float32)
    rhs = jnp.transpose(rhs, (0, 1, 3, 2))
    wave_x = 2.0 * jnp.sin(math.pi * jnp.arange(NX, dtype=jnp.int32).astype(jnp.float32) / NX)
    wave_y = 2.0 * jnp.sin(math.pi * jnp.arange(NY, dtype=jnp.int32).astype(jnp.float32) / NY)
    wave = wave_y[:, None] * wave_y[:, None] + wave_x[None, :] * wave_x[None, :]
    lateral, couple = couplings(layer_kind, permit_lateral, permit_normal)
    potential_modes = solve_layers(rhs, wave, lateral, couple)
    return stress_next, velocity_next, potential_modes
```

```python
import functools
import math

import jax
import jax.numpy as jnp
import ml_dtypes
import numpy as np
from jax import lax
from jax.experimental import pallas as pl
from jax.experimental.pallas import tpu as pltpu
from jax.sharding import PartitionSpec as P

NZ = 16
NX = 2048
NY = 1024
DX = 32
DY = 8
BX = NX // DX
BY = NY // DY
VMEM_LIMIT = 56 * 1024 * 1024


def halves(values):
    high = values.astype(ml_dtypes.bfloat16)
    low = (values - high.astype(np.float64)).astype(ml_dtypes.bfloat16)
    return high, low


def split(values):
    high = values.astype(jnp.bfloat16)
    low = (values - high.astype(jnp.float32)).astype(jnp.bfloat16)
    return high, low


def tables_y():
    j = np.arange(128)
    a = np.arange(8)
    angle = 2.0 * np.pi * (np.outer(j, j) % 128) / 128
    cos, sin = np.cos(angle) / 32.0, np.sin(angle) / 32.0
    weights = np.block([[cos, sin], [-sin, cos]])
    turn = 2.0 * np.pi * np.outer(a, j) / NY
    twiddle = np.stack([np.cos(turn), np.sin(turn)], axis=1).reshape(16, 128)
    return *halves(weights), twiddle.astype(np.float32)


def tables_x():
    n1 = np.arange(128)
    angle = 2.0 * np.pi * (np.outer(n1, n1) % 128) / 128
    scale = 1.0 / math.sqrt(NX)
    cos, sin = np.cos(angle) * scale, np.sin(angle) * scale
    real_rows = np.concatenate([cos, -sin], axis=1).reshape(DX, 1, 4, 256)
    imag_rows = np.concatenate([sin, cos], axis=1).reshape(DX, 1, 4, 256)
    weights = np.concatenate([real_rows, imag_rows], axis=1).reshape(256, 256)
    turn = 2.0 * np.pi * np.outer(np.arange(16), n1) / NX
    twiddle = np.stack([np.cos(turn), np.sin(turn)], axis=1).reshape(32, 128)
    return *halves(weights), twiddle.astype(np.float32)


def table_wave():
    wave = 2.0 * np.sin(np.pi * np.arange(NX) / NX)
    return (wave * wave).astype(np.float32).reshape(1, NX)


def dot3(a, b, dims):
    (a_high, a_low), (b_high, b_low) = a, b
    dot = functools.partial(
        lax.dot_general, dimension_numbers=(dims, ((), ())), preferred_element_type=jnp.float32
    )
    return dot(a_high, b_high) + (dot(a_low, b_high) + dot(a_high, b_low))


def pick(codes, table_ref):
    first, second, third = table_ref[0], table_ref[1], table_ref[2]
    return jnp.where(codes == 0, first, jnp.where(codes == 1, second, third))


def lanes(values):
    return lax.broadcasted_iota(jnp.int32, values.shape, values.ndim - 1)


def rows(values):
    return lax.broadcasted_iota(jnp.int32, values.shape, values.ndim - 2)


def next_lane(values):
    moved = pltpu.roll(values, values.shape[-1] - 1, values.ndim - 1)
    return jnp.where(lanes(values) == values.shape[-1] - 1, 0.0, moved)


def last_lane(values):
    moved = pltpu.roll(values, 1, values.ndim - 1)
    return jnp.where(lanes(values) == 0, 0.0, moved)


def next_row(values, edge):
    size = values.shape[0]
    moved = pltpu.roll(values, size - 1, 0)
    tail = moved[size - 8 :]
    tail = jnp.where(rows(tail) == 7, edge, tail)
    return jnp.concatenate([moved[: size - 8], tail], axis=0)


def last_row(values, edge):
    moved = pltpu.roll(values, 1, 0)
    head = jnp.where(rows(moved[:8]) == 0, edge, moved[:8])
    return jnp.concatenate([head, moved[8:]], axis=0)


def next_layer(values):
    size = values.shape[0]
    moved = pltpu.roll(values, size - 1, 0)
    return jnp.where(rows(values) == size - 1, 0.0, moved)


def last_layer(values):
    moved = pltpu.roll(values, 1, 0)
    return jnp.where(rows(values) == 0, 0.0, moved)


def edge_rows(buoy, stress_first, stress_end, veloc_first, veloc_end, mat_first, mat_end, down_ref, up_ref):
    sxx, sxy, sxz = (stress_end[c, :, 7, :] for c in (0, 3, 4))
    b = pick(mat_end[:, 7, :], buoy)
    down_ref[0] = veloc_end[0, :, 7, :] + b * ((sxy - last_lane(sxy)) + (sxz - last_layer(sxz)) - sxx)
    down_ref[1] = b
    down_ref[2] = sxy
    down_ref[3] = sxz
    sxx, syy, szz, sxy, sxz, syz = (stress_first[c, :, 0, :] for c in range(6))
    b = pick(mat_first[:, 0, :], buoy)
    up_ref[0] = veloc_first[1, :, 0, :] + b * (sxy + (next_lane(syy) - syy) + (syz - last_layer(syz)))
    up_ref[1] = veloc_first[2, :, 0, :] + b * (sxz + (syz - last_lane(syz)) + (next_layer(szz) - szz))
    up_ref[2] = b
    up_ref[3] = sxx
    up_ref[4] = syy
    up_ref[5] = syz


def advance_velocity(buoy, stress, veloc, material, low, high, new, right_ref, left_ref):
    column = lax.broadcasted_iota(jnp.int32, (BX, BY), 1)
    right = jnp.zeros((BX, BY), jnp.float32)
    left = jnp.zeros((BX, BY), jnp.float32)
    for z in range(NZ):
        sxx, syy, szz, sxy, sxz, syz = (stress[c, z] for c in range(6))
        b = pick(material[z], buoy)
        dz_sxz = sxz - stress[4, z - 1] if z else sxz
        dz_syz = syz - stress[5, z - 1] if z else syz
        dz_szz = stress[2, z + 1] - szz if z < NZ - 1 else -szz
        ux = veloc[0, z] + b * (
            (next_row(sxx, high[3, z : z + 1]) - sxx) + (sxy - last_lane(sxy)) + dz_sxz
        )
        uy = veloc[1, z] + b * (
            (sxy - last_row(sxy, low[2, z : z + 1])) + (next_lane(syy) - syy) + dz_syz
        )
        uz = veloc[2, z] + b * (
            (sxz - last_row(sxz, low[3, z : z + 1])) + (syz - last_lane(syz)) + dz_szz
        )
        new[0, z] = ux
        new[1, z] = uy
        new[2, z] = uz
        for part, value in enumerate((uy, b, sxy, syz)):
            spot = part * NZ + z
            moved = pltpu.roll(value, (spot + 1) % BY, 1)
            right = jnp.where(column == spot, moved, right)
        for part, value in enumerate((ux, uz, b, syy)):
            spot = part * NZ + z
            moved = pltpu.roll(value, spot, 1) if spot else value
            left = jnp.where(column == spot, moved, left)
    right_ref[:BX] = right
    left_ref[:BX] = left
    corner = column[:NZ]
    right_ref[BX:] = jnp.where(
        corner == 0, pltpu.roll(low[2], 1, 1), jnp.where(corner == 1, pltpu.roll(high[5], 2, 1), 0.0)
    )
    left_ref[BX:] = jnp.where(corner == 0, high[4], 0.0)


def advance_stress(
    buoy, lame, shear, piezo, stress, part, material, low, high,
    own_right, own_left, from_left, from_right, new_stress, new_veloc, charge,
):
    lane = lax.broadcasted_iota(jnp.int32, (BX, BY), 1)
    corner_lane = lane[:NZ]
    west, east = from_left[:BX], from_right[:BX]
    mine_east, mine_west = own_right[:BX], own_left[:BX]

    def shifted(values, by):
        return pltpu.roll(values, (-by * NZ) % BY, 1)

    uy_west = west + shifted(west, 1) * shifted(mine_west, 3)
    ux_east = east - shifted(east, 2) * shifted(mine_east, 2)
    uz_east = shifted(east, 1) - shifted(east, 2) * shifted(mine_east, 3)
    west_corner, east_corner = from_left[BX:], from_right[BX:]
    ux_low = low[0] - jnp.where(corner_lane == 0, low[1] * west_corner[:, 0:1], 0.0)
    uy_high = high[0] + jnp.where(corner_lane == BY - 1, high[2] * east_corner[:, 0:1], 0.0)
    uz_high = high[1] - jnp.where(corner_lane == 0, high[2] * west_corner[:, 1:2], 0.0)

    def beside(values, spot):
        return jnp.broadcast_to(values[:, spot : spot + 1], (BX, BY))

    for z in range(NZ):
        b = pick(material[z], buoy)
        new_veloc[0, z] = part[0, z] - jnp.where(lane == 0, b * beside(west, 2 * NZ + z), 0.0)
        new_veloc[1, z] = part[1, z] + jnp.where(lane == BY - 1, b * beside(east, 3 * NZ + z), 0.0)
        new_veloc[2, z] = part[2, z] - jnp.where(lane == 0, b * beside(west, 3 * NZ + z), 0.0)
    for z in range(NZ):
        sxx, syy, szz, sxy, sxz, syz = (stress[c, z] for c in range(6))
        ux, uy, uz = (new_veloc[c, z] for c in range(3))
        codes = material[z]
        lam, mu, e = pick(codes, lame), pick(codes, shear), pick(codes, piezo)
        row = slice(z, z + 1)
        ex = ux - last_row(ux, ux_low[row] + low[1, row] * sxx[0:1])
        ey = uy - jnp.where(lane == 0, beside(uy_west, z), pltpu.roll(uy, 1, 1))
        ez = uz - new_veloc[2, z - 1] if z else uz
        lam_div = lam * (ex + ey + ez)
        mu2 = 2.0 * mu
        new_stress[0, z] = sxx + lam_div + mu2 * ex
        new_stress[1, z] = syy + lam_div + mu2 * ey
        new_stress[2, z] = szz + lam_div + mu2 * ez
        b_high = high[2, row]
        dx_uy = next_row(uy, uy_high[row] - b_high * sxy[BX - 1 : BX]) - uy
        dx_uz = next_row(uz, uz_high[row] - b_high * sxz[BX - 1 : BX]) - uz
        last = lane == BY - 1
        dy_ux = jnp.where(last, beside(ux_east, z), pltpu.roll(ux, BY - 1, 1)) - ux
        dy_uz = jnp.where(last, beside(uz_east, z), pltpu.roll(uz, BY - 1, 1)) - uz
        dz_ux = new_veloc[0, z + 1] - ux if z < NZ - 1 else -ux
        dz_uy = new_veloc[1, z + 1] - uy if z < NZ - 1 else -uy
        new_sxz = sxz + mu * (dz_ux + dx_uz)
        new_syz = syz + mu * (dz_uy + dy_uz)
        new_stress[3, z] = sxy + mu * (dy_ux + dx_uy)
        new_stress[4, z] = new_sxz
        new_stress[5, z] = new_syz
        charge[z] = e * (new_sxz + new_syz)


ROOT = math.sqrt(0.5)


def real_dft8(c):
    s = [c[i] + c[i + 4] for i in range(4)]
    d = [c[i] - c[i + 4] for i in range(4)]
    even, odd = s[0] + s[2], s[1] + s[3]
    near, far = ROOT * (d[1] - d[3]), ROOT * (d[1] + d[3])
    re1, re3 = d[0] + near, d[0] - near
    im1, im3 = -(d[2] + far), d[2] - far
    re2, im2 = s[0] - s[2], s[3] - s[1]
    zero = None
    return [
        (even + odd, zero), (re1, im1), (re2, im2), (re3, im3),
        (even - odd, zero), (re3, -im3), (re2, -im2), (re1, -im1),
    ]


def transform_y(charge, w_high, w_low, twiddle, out, real_lines, imag_lines):
    for z in range(2):
        for ihi in range(4):
            at = slice(16 * ihi, 16 * ihi + 16)
            modes = real_dft8([charge[g, z, at, :] for g in range(8)])
            for a, (re, im) in enumerate(modes):
                cos, sin = twiddle[2 * a : 2 * a + 1, :], twiddle[2 * a + 1 : 2 * a + 2, :]
                if a == 0:
                    new_re, new_im = re, jnp.zeros_like(re)
                elif im is None:
                    new_re, new_im = re * cos, -(re * sin)
                else:
                    new_re, new_im = re * cos + im * sin, im * cos - re * sin
                base = (ihi * 2 + a // 4) * 128 + z * 4 + a % 4
                real_lines[pl.ds(base, 16, stride=8), :] = new_re
                imag_lines[pl.ds(base, 16, stride=8), :] = new_im
    weights = (w_high[...], w_low[...])
    for ihi in range(4):
        for ahi in range(2):
            block = slice((ihi * 2 + ahi) * 128, (ihi * 2 + ahi + 1) * 128)
            lines = jnp.concatenate([real_lines[block, :], imag_lines[block, :]], axis=1)
            modes = dot3(weights, split(lines), ((1,), (1,)))
            for part in range(2):
                start = ahi * 8 + part * 4 + ihi
                out[pl.ds(start, 128, stride=16), :] = modes[part * 128 : (part + 1) * 128]


def butterfly4(x):
    (ar, ai), (br, bi) = (
        (x[0][0] + x[2][0], x[0][1] + x[2][1]),
        (x[0][0] - x[2][0], x[0][1] - x[2][1]),
    )
    (cr, ci), (dr, di) = (
        (x[1][0] + x[3][0], x[1][1] + x[3][1]),
        (x[1][0] - x[3][0], x[1][1] - x[3][1]),
    )
    return [(ar + cr, ai + ci), (br + di, bi - dr), (ar - cr, ai - ci), (br - di, bi + dr)]


def turned(value, step):
    re, im = value
    step %= 16
    if step == 0:
        return value
    if step == 4:
        return im, -re
    if step == 2:
        return ROOT * (re + im), ROOT * (im - re)
    if step == 6:
        return ROOT * (im - re), -ROOT * (re + im)
    cos, sin = math.cos(2 * math.pi * step / 16), math.sin(2 * math.pi * step / 16)
    return re * cos + im * sin, im * cos - re * sin


def dft16(x):
    inner = [butterfly4([x[4 * na + nb] for na in range(4)]) for nb in range(4)]
    result = [None] * 16
    for ka in range(4):
        outer = butterfly4([turned(inner[nb][ka], nb * ka) for nb in range(4)])
        for kb in range(4):
            result[ka + 4 * kb] = outer[kb]
    return result


def coupling_scalars(layer_kind, lateral, normal):
    def at(table, kind):
        return jnp.where(kind == 0, table[0], jnp.where(kind == 1, table[1], table[2]))

    el = [at(lateral, layer_kind[z]) for z in range(NZ)]
    en = [at(normal, layer_kind[z]) for z in range(NZ)]
    g = [en[0]] + [0.5 * (en[z - 1] + en[z]) for z in range(1, NZ)] + [en[-1]]
    return el, g


def pivots(layer_kind, lateral, normal, wave_x, inverse):
    el, g = coupling_scalars(layer_kind, lateral, normal)
    first = (lax.axis_index("gx") * DY + lax.axis_index("gy")) * 4
    ky = first + rows(jnp.zeros((8, 128), jnp.float32)) % 4
    wave_y = 2.0 * jnp.sin(math.pi * ky.astype(jnp.float32) / NY)
    wave_y = wave_y * wave_y
    for k in range(NX // 512):
        at = slice(512 * k, 512 * k + 512)
        wave = jnp.concatenate([wave_y] * 4, axis=1) + wave_x[:, at]
        factor = None
        for z in range(NZ):
            pivot = g[z] + g[z + 1] + wave * el[z]
            if z:
                pivot = pivot - g[z] * factor
            inv = 1.0 / pivot
            inverse[z, :, at] = inv
            factor = g[z + 1] * inv


def solve(layer_kind, lateral, normal, lines, w_high, w_low, twiddle, inverse, out, rhs):
    weights = (w_high[...], w_low[...])
    upper = rows(jnp.zeros((8, 128), jnp.float32)) < 4
    for gy in range(DY):
        block = lines[:, gy].reshape(256, 128)
        modes = dot3(split(block.T), weights, ((1,), (0,)))
        turned_modes = []
        for n2 in range(16):
            re, im = modes[8 * n2 : 8 * n2 + 8, :128], modes[8 * n2 : 8 * n2 + 8, 128:]
            if n2:
                cos, sin = twiddle[2 * n2 : 2 * n2 + 1, :], twiddle[2 * n2 + 1 : 2 * n2 + 2, :]
                re, im = re * cos + im * sin, im * cos - re * sin
            turned_modes.append((re, im))
        for k2, (re, im) in enumerate(dft16(turned_modes)):
            at = slice(128 * k2, 128 * k2 + 128)
            rhs[2 * gy, :, at] = jnp.where(upper, re, pltpu.roll(im, 4, 0))
            rhs[2 * gy + 1, :, at] = jnp.where(upper, pltpu.roll(re, 4, 0), im)
    _, g = coupling_scalars(layer_kind, lateral, normal)
    for k in range(NX // 256):
        at = slice(256 * k, 256 * k + 256)
        sums = []
        for z in range(NZ):
            value = rhs[z, :, at]
            if z:
                value = value + g[z] * (sums[-1] * inverse[z - 1, :, at])
            sums.append(value)
        above = None
        for z in range(NZ - 1, -1, -1):
            value = sums[z]
            if above is not None:
                value = value + g[z + 1] * above
            above = value * inverse[z, :, at]
            out[0, z, :, at] = above[:4]
            out[1, z, :, at] = above[4:]


SMEM = pl.BlockSpec(memory_space=pltpu.SMEM)
VMEM = pl.BlockSpec(memory_space=pltpu.VMEM)


def call(body, name, outs, in_specs, args, scratch=(), flops=1_000_000, grid_spec=None):
    shapes = [jax.ShapeDtypeStruct(shape, jnp.float32) for shape in outs]
    moved = sum(4 * math.prod(shape) for shape in outs) + sum(4 * v.size for v in args)
    return pl.pallas_call(
        body,
        name=name,
        out_shape=shapes,
        in_specs=in_specs,
        out_specs=[VMEM] * len(outs),
        scratch_shapes=list(scratch),
        compiler_params=pltpu.CompilerParams(vmem_limit_bytes=VMEM_LIMIT),
        cost_estimate=pl.CostEstimate(flops=flops, bytes_accessed=moved, transcendentals=0),
    )(*args)


def edge_call(buoyancy, stress, velocity, material):
    end = BX // 8 - 1
    block4 = lambda count, at: pl.BlockSpec((count, NZ, 8, BY), lambda i: (0, 0, at, 0))
    block3 = lambda at: pl.BlockSpec((NZ, 8, BY), lambda i: (0, at, 0))
    whole = lambda count: pl.BlockSpec((count, NZ, BY), lambda i: (0, 0, 0))
    return pl.pallas_call(
        edge_rows,
        name="edge_rows",
        grid=(1,),
        out_shape=[jax.ShapeDtypeStruct((count, NZ, BY), jnp.float32) for count in (4, 6)],
        in_specs=[SMEM, block4(6, 0), block4(6, end), block4(3, 0), block4(3, end), block3(0), block3(end)],
        out_specs=[whole(4), whole(6)],
        compiler_params=pltpu.CompilerParams(vmem_limit_bytes=VMEM_LIMIT),
    )(buoyancy, stress, stress, velocity, velocity, material, material)


def per_device(
    stress, velocity, material, layer_kind, buoyancy, lame_first, shear_modulus, piezo, permit_lateral, permit_normal
):
    def chain(count):
        forward = [(i, i + 1) for i in range(count - 1)]
        return forward, [(target, source) for source, target in forward]

    down, up = chain(DX)
    right, left = chain(DY)
    to_next, to_previous = edge_call(buoyancy, stress, velocity, material)
    low = lax.ppermute(to_next, "gx", down)
    high = lax.ppermute(to_previous, "gx", up)
    part, own_right, own_left = call(
        advance_velocity,
        "advance_velocity",
        [(3, NZ, BX, BY), (BX + NZ, BY), (BX + NZ, BY)],
        [SMEM] + [VMEM] * 5,
        (buoyancy, stress, velocity, material, low, high),
    )
    from_left = lax.ppermute(own_right, "gy", right)
    from_right = lax.ppermute(own_left, "gy", left)
    stress_next, velocity_next, charge = call(
        advance_stress,
        "advance_stress",
        [(6, NZ, BX, BY), (3, NZ, BX, BY), (NZ, BX, BY)],
        [SMEM] * 4 + [VMEM] * 9,
        (
            buoyancy, lame_first, shear_modulus, piezo, stress, part, material, low, high,
            own_right, own_left, from_left, from_right,
        ),
    )
    charge = lax.all_to_all(charge, "gy", 0, 0, tiled=True).reshape(DY, 2, BX, BY)
    modes, = call(
        transform_y,
        "transform_y",
        [(NY * 2, 128)],
        [VMEM] * 4,
        (charge, *(jnp.asarray(t) for t in tables_y())),
        [pltpu.VMEM((1024, 128), jnp.float32)] * 2,
    )
    lines = lax.all_to_all(modes.reshape(DX * DY, 8, 128), ("gx", "gy"), 0, 0, tiled=True)
    scalars = (layer_kind, permit_lateral, permit_normal)
    inverse, = call(
        pivots, "pivots", [(NZ, 8, NX)], [SMEM] * 3 + [VMEM], (*scalars, jnp.asarray(table_wave()))
    )
    potential_modes, = call(
        solve,
        "solve",
        [(2, NZ, 4, NX)],
        [SMEM] * 3 + [VMEM] * 5,
        (*scalars, lines.reshape(DX, DY, 8, 128), *(jnp.asarray(t) for t in tables_x()), inverse),
        [pltpu.VMEM((NZ, 8, NX), jnp.float32)],
    )
    return (stress_next, velocity_next, potential_modes)


def solution(mesh):
    field = P(None, None, "gx", "gy")
    return jax.shard_map(
        per_device,
        mesh=mesh,
        in_specs=(field, field, P(None, "gx", "gy")) + (P(),) * 7,
        out_specs=(field, field, P(None, None, ("gx", "gy"), None)),
        check_vma=False,
    )
```

```python
import functools
import math

import jax
import jax.numpy as jnp
import ml_dtypes
import numpy as np
from jax import lax
from jax.experimental import pallas as pl
from jax.experimental.pallas import tpu as pltpu
from jax.sharding import PartitionSpec as P

NZ = 16
NX = 2048
NY = 1024
DX = 32
DY = 8
BX = NX // DX
BY = NY // DY
VMEM_LIMIT = 56 * 1024 * 1024


def halves(values):
    high = values.astype(ml_dtypes.bfloat16)
    low = (values - high.astype(np.float64)).astype(ml_dtypes.bfloat16)
    return high, low


def split(values):
    high = values.astype(jnp.bfloat16)
    low = (values - high.astype(jnp.float32)).astype(jnp.bfloat16)
    return high, low


def tables_y():
    j = np.arange(128)
    a = np.arange(8)
    angle = 2.0 * np.pi * (np.outer(j, j) % 128) / 128
    cos, sin = np.cos(angle) / 32.0, np.sin(angle) / 32.0
    weights = np.block([[cos, sin], [-sin, cos]])
    turn = 2.0 * np.pi * np.outer(a, j) / NY
    twiddle = np.stack([np.cos(turn), np.sin(turn)], axis=1).reshape(16, 128)
    return *halves(weights), twiddle.astype(np.float32)


def tables_x():
    n1 = np.arange(128)
    angle = 2.0 * np.pi * (np.outer(n1, n1) % 128) / 128
    scale = 1.0 / math.sqrt(NX)
    cos, sin = np.cos(angle) * scale, np.sin(angle) * scale
    real_rows = np.concatenate([cos, -sin], axis=1).reshape(DX, 1, 4, 256)
    imag_rows = np.concatenate([sin, cos], axis=1).reshape(DX, 1, 4, 256)
    weights = np.concatenate([real_rows, imag_rows], axis=1).reshape(256, 256)
    turn = 2.0 * np.pi * np.outer(np.arange(16), n1) / NX
    twiddle = np.stack([np.cos(turn), np.sin(turn)], axis=1).reshape(32, 128)
    return *halves(weights), twiddle.astype(np.float32)


def table_wave():
    wave = 2.0 * np.sin(np.pi * np.arange(NX) / NX)
    return (wave * wave).astype(np.float32).reshape(1, NX)


def dot3(a, b, dims):
    (a_high, a_low), (b_high, b_low) = a, b
    dot = functools.partial(
        lax.dot_general, dimension_numbers=(dims, ((), ())), preferred_element_type=jnp.float32
    )
    return dot(a_high, b_high) + (dot(a_low, b_high) + dot(a_high, b_low))


def pick(codes, table_ref):
    first, second, third = table_ref[0], table_ref[1], table_ref[2]
    return jnp.where(codes == 0, first, jnp.where(codes == 1, second, third))


def lanes(values):
    return lax.broadcasted_iota(jnp.int32, values.shape, values.ndim - 1)


def rows(values):
    return lax.broadcasted_iota(jnp.int32, values.shape, values.ndim - 2)


def next_lane(values):
    moved = pltpu.roll(values, values.shape[-1] - 1, values.ndim - 1)
    return jnp.where(lanes(values) == values.shape[-1] - 1, 0.0, moved)


def last_lane(values):
    moved = pltpu.roll(values, 1, values.ndim - 1)
    return jnp.where(lanes(values) == 0, 0.0, moved)


def next_row(values, edge):
    size = values.shape[0]
    moved = pltpu.roll(values, size - 1, 0)
    tail = moved[size - 8 :]
    tail = jnp.where(rows(tail) == 7, edge, tail)
    return jnp.concatenate([moved[: size - 8], tail], axis=0)


def last_row(values, edge):
    moved = pltpu.roll(values, 1, 0)
    head = jnp.where(rows(moved[:8]) == 0, edge, moved[:8])
    return jnp.concatenate([head, moved[8:]], axis=0)


def next_layer(values):
    size = values.shape[0]
    moved = pltpu.roll(values, size - 1, 0)
    return jnp.where(rows(values) == size - 1, 0.0, moved)


def last_layer(values):
    moved = pltpu.roll(values, 1, 0)
    return jnp.where(rows(values) == 0, 0.0, moved)


def odd(axis):
    return lax.axis_index(axis) % 2 == 1


def low_high(axis, first, second):
    is_odd = odd(axis)
    low = [jnp.where(is_odd, first[c], second[c]) for c in range(first.shape[0])]
    high = [jnp.where(is_odd, second[c], first[c]) for c in range(first.shape[0])]
    return low, high


def edge_rows(buoy, stress_first, stress_end, veloc_first, veloc_end, mat_first, mat_end, first, second):
    sxx, sxy, sxz = (stress_end[c, :, 7, :] for c in (0, 3, 4))
    b = pick(mat_end[:, 7, :], buoy)
    ux = veloc_end[0, :, 7, :] + b * ((sxy - last_lane(sxy)) + (sxz - last_layer(sxz)) - sxx)
    down = [ux, b, sxy, sxz, jnp.zeros_like(b), jnp.zeros_like(b)]
    sxx, syy, szz, sxy, sxz, syz = (stress_first[c, :, 0, :] for c in range(6))
    b = pick(mat_first[:, 0, :], buoy)
    uy = veloc_first[1, :, 0, :] + b * (sxy + (next_lane(syy) - syy) + (syz - last_layer(syz)))
    uz = veloc_first[2, :, 0, :] + b * (sxz + (syz - last_lane(syz)) + (next_layer(szz) - szz))
    up = [uy, uz, b, sxx, syy, syz]
    is_odd = odd("gx")
    for c in range(6):
        first[c] = jnp.where(is_odd, up[c], down[c])
        second[c] = jnp.where(is_odd, down[c], up[c])


CHUNK = 2


def copies(pairs, sems):
    made = []
    for k in range(NZ // CHUNK):
        at = pl.ds(k * CHUNK, CHUNK)
        made.append([])
        for n, (source, target) in enumerate(pairs):
            index = (at,) if len(source.shape) == 3 else (slice(None), at)
            made[-1].append(pltpu.make_async_copy(source.at[index], target.at[index], sems.at[k, n]))
    return made


def advance_velocity(
    buoy, stress_in, veloc_in, material_in, new_out, right_ref, left_ref,
    stress, veloc, material, new, in_sems, out_sems,
):
    arriving = copies([(stress_in, stress), (veloc_in, veloc), (material_in, material)], in_sems)
    leaving = copies([(new, new_out)], out_sems)
    for chunk in arriving:
        for copy in chunk:
            copy.start()
    column = lax.broadcasted_iota(jnp.int32, (BX, BY), 1)
    right = jnp.zeros((BX, BY), jnp.float32)
    left = jnp.zeros((BX, BY), jnp.float32)
    ready = 0
    for z in range(NZ):
        while ready < min(z + 2, NZ):
            for copy in arriving[ready // CHUNK]:
                copy.wait()
            ready += CHUNK
        sxx, syy, szz, sxy, sxz, syz = (stress[c, z] for c in range(6))
        b = pick(material[z], buoy)
        dz_sxz = sxz - stress[4, z - 1] if z else sxz
        dz_syz = syz - stress[5, z - 1] if z else syz
        dz_szz = stress[2, z + 1] - szz if z < NZ - 1 else -szz
        ux = veloc[0, z] + b * ((next_row(sxx, 0.0) - sxx) + (sxy - last_lane(sxy)) + dz_sxz)
        uy = veloc[1, z] + b * ((sxy - last_row(sxy, 0.0)) + (next_lane(syy) - syy) + dz_syz)
        uz = veloc[2, z] + b * ((sxz - last_row(sxz, 0.0)) + (syz - last_lane(syz)) + dz_szz)
        new[0, z] = ux
        new[1, z] = uy
        new[2, z] = uz
        if z % CHUNK == CHUNK - 1:
            for copy in leaving[z // CHUNK]:
                copy.start()
        for part, value in enumerate((uy, b, sxy, syz)):
            spot = part * NZ + z
            moved = pltpu.roll(value, (spot + 1) % BY, 1)
            right = jnp.where(column == spot, moved, right)
        for part, value in enumerate((ux, uz, b, syy)):
            spot = part * NZ + z
            moved = pltpu.roll(value, spot, 1) if spot else value
            left = jnp.where(column == spot, moved, left)
    right_ref[...] = right
    left_ref[...] = left
    for chunk in leaving:
        for copy in chunk:
            copy.wait()


def edge_columns(right_ref, left_ref, x_first, x_second, first, second):
    low, high = low_high("gx", x_first, x_second)
    corner = lax.broadcasted_iota(jnp.int32, (NZ, BY), 1)
    layer = lax.broadcasted_iota(jnp.int32, (NZ, BY), 0)
    row = lax.broadcasted_iota(jnp.int32, (BX, BY), 0)
    column = lax.broadcasted_iota(jnp.int32, (BX, BY), 1)

    def line(values, spot, at):
        wide = jnp.broadcast_to(values[:, spot : spot + 1], (NZ, BY))
        return jnp.sum(jnp.where(corner == layer + at, wide, 0.0), axis=0, keepdims=True)

    def shifted(values, by):
        return pltpu.roll(values, (-by * NZ) % BY, 1)

    right, left = right_ref[...], left_ref[...]
    right_b = shifted(right, 1)
    right = right - jnp.where((row == 0) & (column < NZ), right_b * line(low[2], BY - 1, 0), 0.0)
    left_b = jnp.where(column < NZ, shifted(left, 2), shifted(left, 1))
    left = left + jnp.where((row == BX - 1) & (column < NZ), left_b * line(high[3], 0, 0), 0.0)
    left = left - jnp.where(
        (row == 0) & (column >= NZ) & (column < 2 * NZ), left_b * line(low[3], 0, NZ), 0.0
    )
    right_corner = jnp.where(
        corner == 0, pltpu.roll(low[2], 1, 1), jnp.where(corner == 1, pltpu.roll(high[5], 2, 1), 0.0)
    )
    left_corner = jnp.where(corner == 0, high[4], 0.0)
    is_odd = odd("gy")
    first[:BX] = jnp.where(is_odd, left, right)
    first[BX:] = jnp.where(is_odd, left_corner, right_corner)
    second[:BX] = jnp.where(is_odd, right, left)
    second[BX:] = jnp.where(is_odd, right_corner, left_corner)


def advance_stress(
    buoy, lame, shear, piezo, stress_in, part_in, material_in, x_first, x_second,
    own_right, own_left, y_first, y_second, stress_out, veloc_out, charge_out,
    stress, part, material, new_stress, new_veloc, charge, in_sems, out_sems,
):
    arriving = copies([(stress_in, stress), (part_in, part), (material_in, material)], in_sems)
    leaving = copies([(charge, charge_out), (new_stress, stress_out), (new_veloc, veloc_out)], out_sems)
    for chunk in arriving:
        for copy in chunk:
            copy.start()
    lane = lax.broadcasted_iota(jnp.int32, (BX, BY), 1)
    corner_lane = lane[:NZ]
    row8 = lax.broadcasted_iota(jnp.int32, (8, BY), 0)
    low, high = low_high("gx", x_first, x_second)
    y_odd = odd("gy")
    from_left = jnp.where(y_odd, y_first[...], y_second[...])
    from_right = jnp.where(y_odd, y_second[...], y_first[...])
    west, east = from_left[:BX], from_right[:BX]
    mine_east, mine_west = own_right[...], own_left[...]

    def shifted(values, by):
        return pltpu.roll(values, (-by * NZ) % BY, 1)

    uy_west = west + shifted(west, 1) * shifted(mine_west, 3)
    ux_east = east - shifted(east, 2) * shifted(mine_east, 2)
    uz_east = shifted(east, 1) - shifted(east, 2) * shifted(mine_east, 3)
    west_corner, east_corner = from_left[BX:], from_right[BX:]
    ux_low = low[0] - jnp.where(corner_lane == 0, low[1] * west_corner[:, 0:1], 0.0)
    uy_high = high[0] + jnp.where(corner_lane == BY - 1, high[2] * east_corner[:, 0:1], 0.0)
    uz_high = high[1] - jnp.where(corner_lane == 0, high[2] * west_corner[:, 1:2], 0.0)

    def beside(values, spot):
        return jnp.broadcast_to(values[:, spot : spot + 1], (BX, BY))

    def at_top(values, added):
        head = values[:8] + jnp.where(row8 == 0, added, 0.0)
        return jnp.concatenate([head, values[8:]], axis=0)

    def at_end(values, added):
        tail = values[BX - 8 :] + jnp.where(row8 == 7, added, 0.0)
        return jnp.concatenate([values[: BX - 8], tail], axis=0)

    def close_edges(z):
        b = pick(material[z], buoy)
        row = slice(z, z + 1)
        head, tail = b[:8], b[BX - 8 :]
        ux = part[0, z] - jnp.where(lane == 0, b * beside(west, 2 * NZ + z), 0.0)
        uy = part[1, z] + jnp.where(lane == BY - 1, b * beside(east, 3 * NZ + z), 0.0)
        uz = part[2, z] - jnp.where(lane == 0, b * beside(west, 3 * NZ + z), 0.0)
        new_veloc[0, z] = at_end(ux, tail * high[3][row])
        new_veloc[1, z] = at_top(uy, -(head * low[2][row]))
        new_veloc[2, z] = at_top(uz, -(head * low[3][row]))

    ready = 0
    for step in range(NZ + 1):
        if step < NZ:
            while ready <= step:
                for copy in arriving[ready // CHUNK]:
                    copy.wait()
                ready += CHUNK
            close_edges(step)
        if step == 0:
            continue
        z = step - 1
        sxx, syy, szz, sxy, sxz, syz = (stress[c, z] for c in range(6))
        ux, uy, uz = (new_veloc[c, z] for c in range(3))
        codes = material[z]
        lam, mu, e = pick(codes, lame), pick(codes, shear), pick(codes, piezo)
        row = slice(z, z + 1)
        ex = ux - last_row(ux, ux_low[row] + low[1][row] * sxx[0:1])
        ey = uy - jnp.where(lane == 0, beside(uy_west, z), pltpu.roll(uy, 1, 1))
        ez = uz - new_veloc[2, z - 1] if z else uz
        lam_div = lam * (ex + ey + ez)
        mu2 = 2.0 * mu
        new_stress[0, z] = sxx + lam_div + mu2 * ex
        new_stress[1, z] = syy + lam_div + mu2 * ey
        new_stress[2, z] = szz + lam_div + mu2 * ez
        b_high = high[2][row]
        dx_uy = next_row(uy, uy_high[row] - b_high * sxy[BX - 1 : BX]) - uy
        dx_uz = next_row(uz, uz_high[row] - b_high * sxz[BX - 1 : BX]) - uz
        last = lane == BY - 1
        dy_ux = jnp.where(last, beside(ux_east, z), pltpu.roll(ux, BY - 1, 1)) - ux
        dy_uz = jnp.where(last, beside(uz_east, z), pltpu.roll(uz, BY - 1, 1)) - uz
        dz_ux = new_veloc[0, z + 1] - ux if z < NZ - 1 else -ux
        dz_uy = new_veloc[1, z + 1] - uy if z < NZ - 1 else -uy
        new_sxz = sxz + mu * (dz_ux + dx_uz)
        new_syz = syz + mu * (dz_uy + dy_uz)
        new_stress[3, z] = sxy + mu * (dy_ux + dx_uy)
        new_stress[4, z] = new_sxz
        new_stress[5, z] = new_syz
        charge[z] = e * (new_sxz + new_syz)
        if z % CHUNK == CHUNK - 1:
            for copy in leaving[z // CHUNK]:
                copy.start()
    for chunk in leaving:
        for copy in chunk:
            copy.wait()


ROOT = math.sqrt(0.5)


def real_dft8(c):
    s = [c[i] + c[i + 4] for i in range(4)]
    d = [c[i] - c[i + 4] for i in range(4)]
    even, odd = s[0] + s[2], s[1] + s[3]
    near, far = ROOT * (d[1] - d[3]), ROOT * (d[1] + d[3])
    re1, re3 = d[0] + near, d[0] - near
    im1, im3 = -(d[2] + far), d[2] - far
    re2, im2 = s[0] - s[2], s[3] - s[1]
    zero = None
    return [
        (even + odd, zero), (re1, im1), (re2, im2), (re3, im3),
        (even - odd, zero), (re3, -im3), (re2, -im2), (re1, -im1),
    ]


def transform_y(charge, w_high, w_low, twiddle, out, real_lines, imag_lines):
    for z in range(2):
        for ihi in range(4):
            at = slice(16 * ihi, 16 * ihi + 16)
            modes = real_dft8([charge[g, z, at, :] for g in range(8)])
            for a, (re, im) in enumerate(modes):
                cos, sin = twiddle[2 * a : 2 * a + 1, :], twiddle[2 * a + 1 : 2 * a + 2, :]
                if a == 0:
                    new_re, new_im = re, jnp.zeros_like(re)
                elif im is None:
                    new_re, new_im = re * cos, -(re * sin)
                else:
                    new_re, new_im = re * cos + im * sin, im * cos - re * sin
                base = (ihi * 2 + a // 4) * 128 + z * 4 + a % 4
                real_lines[pl.ds(base, 16, stride=8), :] = new_re
                imag_lines[pl.ds(base, 16, stride=8), :] = new_im
    weights = (w_high[...], w_low[...])
    for ihi in range(4):
        for ahi in range(2):
            block = slice((ihi * 2 + ahi) * 128, (ihi * 2 + ahi + 1) * 128)
            lines = jnp.concatenate([real_lines[block, :], imag_lines[block, :]], axis=1)
            modes = dot3(weights, split(lines), ((1,), (1,)))
            for part in range(2):
                start = ahi * 8 + part * 4 + ihi
                out[pl.ds(start, 128, stride=16), :] = modes[part * 128 : (part + 1) * 128]


def butterfly4(x):
    (ar, ai), (br, bi) = (
        (x[0][0] + x[2][0], x[0][1] + x[2][1]),
        (x[0][0] - x[2][0], x[0][1] - x[2][1]),
    )
    (cr, ci), (dr, di) = (
        (x[1][0] + x[3][0], x[1][1] + x[3][1]),
        (x[1][0] - x[3][0], x[1][1] - x[3][1]),
    )
    return [(ar + cr, ai + ci), (br + di, bi - dr), (ar - cr, ai - ci), (br - di, bi + dr)]


def turned(value, step):
    re, im = value
    step %= 16
    if step == 0:
        return value
    if step == 4:
        return im, -re
    if step == 2:
        return ROOT * (re + im), ROOT * (im - re)
    if step == 6:
        return ROOT * (im - re), -ROOT * (re + im)
    cos, sin = math.cos(2 * math.pi * step / 16), math.sin(2 * math.pi * step / 16)
    return re * cos + im * sin, im * cos - re * sin


def dft16(x):
    inner = [butterfly4([x[4 * na + nb] for na in range(4)]) for nb in range(4)]
    result = [None] * 16
    for ka in range(4):
        outer = butterfly4([turned(inner[nb][ka], nb * ka) for nb in range(4)])
        for kb in range(4):
            result[ka + 4 * kb] = outer[kb]
    return result


def coupling_scalars(layer_kind, lateral, normal):
    def at(table, kind):
        return jnp.where(kind == 0, table[0], jnp.where(kind == 1, table[1], table[2]))

    el = [at(lateral, layer_kind[z]) for z in range(NZ)]
    en = [at(normal, layer_kind[z]) for z in range(NZ)]
    g = [en[0]] + [0.5 * (en[z - 1] + en[z]) for z in range(1, NZ)] + [en[-1]]
    return el, g


def pivots(layer_kind, lateral, normal, wave_x, inverse):
    el, g = coupling_scalars(layer_kind, lateral, normal)
    first = (lax.axis_index("gx") * DY + lax.axis_index("gy")) * 4
    ky = first + rows(jnp.zeros((8, 128), jnp.float32)) % 4
    wave_y = 2.0 * jnp.sin(math.pi * ky.astype(jnp.float32) / NY)
    wave_y = wave_y * wave_y
    for k in range(NX // 512):
        at = slice(512 * k, 512 * k + 512)
        wave = jnp.concatenate([wave_y] * 4, axis=1) + wave_x[:, at]
        factor = None
        for z in range(NZ):
            pivot = g[z] + g[z + 1] + wave * el[z]
            if z:
                pivot = pivot - g[z] * factor
            inv = 1.0 / pivot
            inverse[z, :, at] = inv
            factor = g[z + 1] * inv


def solve(layer_kind, lateral, normal, lines, w_high, w_low, twiddle, inverse, out, rhs):
    weights = (w_high[...], w_low[...])
    upper = rows(jnp.zeros((8, 128), jnp.float32)) < 4
    for gy in range(DY):
        block = lines[:, gy].reshape(256, 128)
        modes = dot3(split(block.T), weights, ((1,), (0,)))
        turned_modes = []
        for n2 in range(16):
            re, im = modes[8 * n2 : 8 * n2 + 8, :128], modes[8 * n2 : 8 * n2 + 8, 128:]
            if n2:
                cos, sin = twiddle[2 * n2 : 2 * n2 + 1, :], twiddle[2 * n2 + 1 : 2 * n2 + 2, :]
                re, im = re * cos + im * sin, im * cos - re * sin
            turned_modes.append((re, im))
        for k2, (re, im) in enumerate(dft16(turned_modes)):
            at = slice(128 * k2, 128 * k2 + 128)
            rhs[2 * gy, :, at] = jnp.where(upper, re, pltpu.roll(im, 4, 0))
            rhs[2 * gy + 1, :, at] = jnp.where(upper, pltpu.roll(re, 4, 0), im)
    _, g = coupling_scalars(layer_kind, lateral, normal)
    for k in range(NX // 256):
        at = slice(256 * k, 256 * k + 256)
        sums = []
        for z in range(NZ):
            value = rhs[z, :, at]
            if z:
                value = value + g[z] * (sums[-1] * inverse[z - 1, :, at])
            sums.append(value)
        above = None
        for z in range(NZ - 1, -1, -1):
            value = sums[z]
            if above is not None:
                value = value + g[z + 1] * above
            above = value * inverse[z, :, at]
            out[0, z, :, at] = above[:4]
            out[1, z, :, at] = above[4:]


SMEM = pl.BlockSpec(memory_space=pltpu.SMEM)
VMEM = pl.BlockSpec(memory_space=pltpu.VMEM)
ANY = pl.BlockSpec(memory_space=pl.ANY)


def call(body, name, outs, in_specs, args, scratch=(), out_specs=None, flops=1_000_000):
    shapes = [jax.ShapeDtypeStruct(shape, jnp.float32) for shape in outs]
    moved = sum(4 * math.prod(shape) for shape in outs) + sum(4 * v.size for v in args)
    return pl.pallas_call(
        body,
        name=name,
        out_shape=shapes,
        in_specs=in_specs,
        out_specs=out_specs or [VMEM] * len(outs),
        scratch_shapes=list(scratch),
        compiler_params=pltpu.CompilerParams(vmem_limit_bytes=VMEM_LIMIT),
        cost_estimate=pl.CostEstimate(flops=flops, bytes_accessed=moved, transcendentals=0),
    )(*args)


def edge_call(buoyancy, stress, velocity, material):
    end = BX // 8 - 1
    block4 = lambda count, at: pl.BlockSpec((count, NZ, 8, BY), lambda i: (0, 0, at, 0))
    block3 = lambda at: pl.BlockSpec((NZ, 8, BY), lambda i: (0, at, 0))
    whole = pl.BlockSpec((6, NZ, BY), lambda i: (0, 0, 0))
    return pl.pallas_call(
        edge_rows,
        name="edge_rows",
        grid=(1,),
        out_shape=[jax.ShapeDtypeStruct((6, NZ, BY), jnp.float32)] * 2,
        in_specs=[SMEM, block4(6, 0), block4(6, end), block4(3, 0), block4(3, end), block3(0), block3(end)],
        out_specs=[whole, whole],
        compiler_params=pltpu.CompilerParams(vmem_limit_bytes=VMEM_LIMIT),
    )(buoyancy, stress, stress, velocity, velocity, material, material)


def field(count, dtype=jnp.float32):
    shape = (NZ, BX, BY)
    return pltpu.VMEM(shape if count == 1 else (count, *shape), dtype)


def swaps(axis, first, second):
    def pairs(start):
        both = [(i, i + 1) for i in range(start, lax.axis_size(axis) - 1, 2)]
        return both + [(b, a) for a, b in both]

    second = lax.ppermute(second, axis, pairs(1))
    return lax.ppermute(first, axis, pairs(0)), second


def per_device(
    stress, velocity, material, layer_kind, buoyancy, lame_first, shear_modulus, piezo, permit_lateral, permit_normal
):
    chunks = NZ // CHUNK
    sems = lambda count: pltpu.SemaphoreType.DMA((chunks, count))
    x_edges = swaps("gx", *edge_call(buoyancy, stress, velocity, material))
    part, own_right, own_left = call(
        advance_velocity,
        "advance_velocity",
        [(3, NZ, BX, BY), (BX, BY), (BX, BY)],
        [SMEM] + [ANY] * 3,
        (buoyancy, stress, velocity, material),
        [field(6), field(3), field(1, jnp.int32), field(3), sems(3), sems(1)],
        [ANY, VMEM, VMEM],
    )
    y_edges = call(
        edge_columns, "edge_columns", [(BX + NZ, BY)] * 2, [VMEM] * 4, (own_right, own_left, *x_edges)
    )
    y_edges = swaps("gy", *y_edges)
    scalars = (layer_kind, permit_lateral, permit_normal)
    own_right, layer_kind = lax.optimization_barrier((own_right, layer_kind))
    inverse, = call(
        pivots,
        "pivots",
        [(NZ, 8, NX)],
        [SMEM] * 3 + [VMEM],
        (layer_kind, permit_lateral, permit_normal, jnp.asarray(table_wave())),
    )
    own_right, inverse = lax.optimization_barrier((own_right, inverse))
    stress_next, velocity_next, charge = call(
        advance_stress,
        "advance_stress",
        [(6, NZ, BX, BY), (3, NZ, BX, BY), (NZ, BX, BY)],
        [SMEM] * 4 + [ANY] * 3 + [VMEM] * 6,
        (
            buoyancy, lame_first, shear_modulus, piezo, stress, part, material,
            *x_edges, own_right, own_left, *y_edges,
        ),
        [field(6), field(3), field(1, jnp.int32), field(6), field(3), field(1), sems(3), sems(3)],
        [ANY] * 3,
    )
    charge = lax.all_to_all(charge, "gy", 0, 0, tiled=True).reshape(DY, 2, BX, BY)
    modes, = call(
        transform_y,
        "transform_y",
        [(NY * 2, 128)],
        [VMEM] * 4,
        (charge, *(jnp.asarray(t) for t in tables_y())),
        [pltpu.VMEM((1024, 128), jnp.float32)] * 2,
    )
    lines = lax.all_to_all(modes.reshape(DX * DY, 8, 128), ("gx", "gy"), 0, 0, tiled=True)
    potential_modes, = call(
        solve,
        "solve",
        [(2, NZ, 4, NX)],
        [SMEM] * 3 + [VMEM] * 5,
        (*scalars, lines.reshape(DX, DY, 8, 128), *(jnp.asarray(t) for t in tables_x()), inverse),
        [pltpu.VMEM((NZ, 8, NX), jnp.float32)],
    )
    return (stress_next, velocity_next, potential_modes)


def solution(mesh):
    spread = P(None, None, "gx", "gy")
    return jax.shard_map(
        per_device,
        mesh=mesh,
        in_specs=(spread, spread, P(None, "gx", "gy")) + (P(),) * 7,
        out_specs=(spread, spread, P(None, None, ("gx", "gy"), None)),
        check_vma=False,
    )
```

```python
import functools
import math

import jax
import jax.numpy as jnp
import ml_dtypes
import numpy as np
from jax import lax
from jax.experimental import pallas as pl
from jax.experimental.pallas import tpu as pltpu
from jax.sharding import PartitionSpec as P

NZ = 16
NX = 2048
NY = 1024
DX = 32
DY = 8
BX = NX // DX
BY = NY // DY
KEPT_LIMIT = 24 * 1024 * 1024


def halves(values):
    high = values.astype(ml_dtypes.bfloat16)
    low = (values - high.astype(np.float64)).astype(ml_dtypes.bfloat16)
    return high, low


def split(values):
    high = values.astype(jnp.bfloat16)
    low = (values - high.astype(jnp.float32)).astype(jnp.bfloat16)
    return high, low


def tables_y():
    j = np.arange(128)
    a = np.arange(8)
    angle = 2.0 * np.pi * (np.outer(j, j) % 128) / 128
    cos, sin = np.cos(angle) / 32.0, np.sin(angle) / 32.0
    weights = np.block([[cos, sin], [-sin, cos]])
    turn = 2.0 * np.pi * np.outer(a, j) / NY
    twiddle = np.stack([np.cos(turn), np.sin(turn)], axis=1).reshape(16, 128)
    return *halves(weights), twiddle.astype(np.float32)


def tables_x():
    n1 = np.arange(128)
    angle = 2.0 * np.pi * (np.outer(n1, n1) % 128) / 128
    scale = 1.0 / math.sqrt(NX)
    cos, sin = np.cos(angle) * scale, np.sin(angle) * scale
    real_rows = np.concatenate([cos, -sin], axis=1).reshape(DX, 1, 4, 256)
    imag_rows = np.concatenate([sin, cos], axis=1).reshape(DX, 1, 4, 256)
    weights = np.concatenate([real_rows, imag_rows], axis=1).reshape(256, 256)
    turn = 2.0 * np.pi * np.outer(np.arange(16), n1) / NX
    twiddle = np.stack([np.cos(turn), np.sin(turn)], axis=1).reshape(32, 128)
    return *halves(weights), twiddle.astype(np.float32)


def table_wave():
    wave = 2.0 * np.sin(np.pi * np.arange(NX) / NX)
    return (wave * wave).astype(np.float32).reshape(1, NX)


def dot3(a, b, dims):
    (a_high, a_low), (b_high, b_low) = a, b
    dot = functools.partial(
        lax.dot_general, dimension_numbers=(dims, ((), ())), preferred_element_type=jnp.float32
    )
    return dot(a_high, b_high) + (dot(a_low, b_high) + dot(a_high, b_low))


def pick(codes, table_ref):
    first, second, third = table_ref[0], table_ref[1], table_ref[2]
    return jnp.where(codes == 0, first, jnp.where(codes == 1, second, third))


def lanes(values):
    return lax.broadcasted_iota(jnp.int32, values.shape, values.ndim - 1)


def rows(values):
    return lax.broadcasted_iota(jnp.int32, values.shape, values.ndim - 2)


def next_lane(values):
    moved = pltpu.roll(values, values.shape[-1] - 1, values.ndim - 1)
    return jnp.where(lanes(values) == values.shape[-1] - 1, 0.0, moved)


def last_lane(values):
    moved = pltpu.roll(values, 1, values.ndim - 1)
    return jnp.where(lanes(values) == 0, 0.0, moved)


def next_row(values, edge):
    size = values.shape[0]
    moved = pltpu.roll(values, size - 1, 0)
    tail = moved[size - 8 :]
    tail = jnp.where(rows(tail) == 7, edge, tail)
    return jnp.concatenate([moved[: size - 8], tail], axis=0)


def last_row(values, edge):
    moved = pltpu.roll(values, 1, 0)
    head = jnp.where(rows(moved[:8]) == 0, edge, moved[:8])
    return jnp.concatenate([head, moved[8:]], axis=0)


def next_layer(values):
    size = values.shape[0]
    moved = pltpu.roll(values, size - 1, 0)
    return jnp.where(rows(values) == size - 1, 0.0, moved)


def last_layer(values):
    moved = pltpu.roll(values, 1, 0)
    return jnp.where(rows(values) == 0, 0.0, moved)


def odd(axis):
    return lax.axis_index(axis) % 2 == 1


def low_high(axis, first, second):
    is_odd = odd(axis)
    low = [jnp.where(is_odd, first[c], second[c]) for c in range(first.shape[0])]
    high = [jnp.where(is_odd, second[c], first[c]) for c in range(first.shape[0])]
    return low, high


def edge_rows(
    buoy, stress_in, veloc_in, material_in, first, second, stress, veloc, material, sems
):
    moves = []
    for n, row in enumerate((0, BX - 1)):
        at = pl.ds(row, 1)
        moves += [
            pltpu.make_async_copy(stress_in.at[:, :, at], stress.at[n], sems.at[n, 0]),
            pltpu.make_async_copy(veloc_in.at[:, :, at], veloc.at[n], sems.at[n, 1]),
            pltpu.make_async_copy(material_in.at[:, at], material.at[n], sems.at[n, 2]),
        ]
    for move in moves:
        move.start()
    for move in moves:
        move.wait()
    sxx, sxy, sxz = (stress[1, c, :, 0, :] for c in (0, 3, 4))
    b = pick(material[1, :, 0, :], buoy)
    ux = veloc[1, 0, :, 0, :] + b * ((sxy - last_lane(sxy)) + (sxz - last_layer(sxz)) - sxx)
    down = [ux, b, sxy, sxz, jnp.zeros_like(b), jnp.zeros_like(b)]
    sxx, syy, szz, sxy, sxz, syz = (stress[0, c, :, 0, :] for c in range(6))
    b = pick(material[0, :, 0, :], buoy)
    uy = veloc[0, 1, :, 0, :] + b * (sxy + (next_lane(syy) - syy) + (syz - last_layer(syz)))
    uz = veloc[0, 2, :, 0, :] + b * (sxz + (syz - last_lane(syz)) + (next_layer(szz) - szz))
    up = [uy, uz, b, sxx, syy, syz]
    is_odd = odd("gx")
    for c in range(6):
        first[c] = jnp.where(is_odd, up[c], down[c])
        second[c] = jnp.where(is_odd, down[c], up[c])


CHUNK = 4


def copies(pairs, sems):
    made = []
    for k in range(NZ // CHUNK):
        at = pl.ds(k * CHUNK, CHUNK)
        made.append([])
        for n, (source, target) in enumerate(pairs):
            index = (at,) if len(source.shape) == 3 else (slice(None), at)
            made[-1].append(pltpu.make_async_copy(source.at[index], target.at[index], sems.at[k, n]))
    return made


def advance_velocity(buoy, stress, veloc, material, new, right_ref, left_ref):
    column = lax.broadcasted_iota(jnp.int32, (BX, BY), 1)
    right = jnp.zeros((BX, BY), jnp.float32)
    left = jnp.zeros((BX, BY), jnp.float32)
    for z in range(NZ):
        sxx, syy, szz, sxy, sxz, syz = (stress[c, z] for c in range(6))
        b = pick(material[z], buoy)
        dz_sxz = sxz - stress[4, z - 1] if z else sxz
        dz_syz = syz - stress[5, z - 1] if z else syz
        dz_szz = stress[2, z + 1] - szz if z < NZ - 1 else -szz
        ux = veloc[0, z] + b * ((next_row(sxx, 0.0) - sxx) + (sxy - last_lane(sxy)) + dz_sxz)
        uy = veloc[1, z] + b * ((sxy - last_row(sxy, 0.0)) + (next_lane(syy) - syy) + dz_syz)
        uz = veloc[2, z] + b * ((sxz - last_row(sxz, 0.0)) + (syz - last_lane(syz)) + dz_szz)
        new[0, z] = ux
        new[1, z] = uy
        new[2, z] = uz
        for part, value in enumerate((uy, b, sxy, syz)):
            spot = part * NZ + z
            moved = pltpu.roll(value, (spot + 1) % BY, 1)
            right = jnp.where(column == spot, moved, right)
        for part, value in enumerate((ux, uz, b, syy)):
            spot = part * NZ + z
            moved = pltpu.roll(value, spot, 1) if spot else value
            left = jnp.where(column == spot, moved, left)
    right_ref[...] = right
    left_ref[...] = left


def edge_columns(right_ref, left_ref, x_first, x_second, first, second):
    low, high = low_high("gx", x_first, x_second)
    corner = lax.broadcasted_iota(jnp.int32, (NZ, BY), 1)
    layer = lax.broadcasted_iota(jnp.int32, (NZ, BY), 0)
    row = lax.broadcasted_iota(jnp.int32, (BX, BY), 0)
    column = lax.broadcasted_iota(jnp.int32, (BX, BY), 1)

    def line(values, spot, at):
        wide = jnp.broadcast_to(values[:, spot : spot + 1], (NZ, BY))
        return jnp.sum(jnp.where(corner == layer + at, wide, 0.0), axis=0, keepdims=True)

    def shifted(values, by):
        return pltpu.roll(values, (-by * NZ) % BY, 1)

    right, left = right_ref[...], left_ref[...]
    right_b = shifted(right, 1)
    right = right - jnp.where((row == 0) & (column < NZ), right_b * line(low[2], BY - 1, 0), 0.0)
    left_b = jnp.where(column < NZ, shifted(left, 2), shifted(left, 1))
    left = left + jnp.where((row == BX - 1) & (column < NZ), left_b * line(high[3], 0, 0), 0.0)
    left = left - jnp.where(
        (row == 0) & (column >= NZ) & (column < 2 * NZ), left_b * line(low[3], 0, NZ), 0.0
    )
    right_corner = jnp.where(
        corner == 0, pltpu.roll(low[2], 1, 1), jnp.where(corner == 1, pltpu.roll(high[5], 2, 1), 0.0)
    )
    left_corner = jnp.where(corner == 0, high[4], 0.0)
    is_odd = odd("gy")
    first[:BX] = jnp.where(is_odd, left, right)
    first[BX:] = jnp.where(is_odd, left_corner, right_corner)
    second[:BX] = jnp.where(is_odd, right, left)
    second[BX:] = jnp.where(is_odd, right_corner, left_corner)


def advance_stress(
    buoy, lame, shear, piezo, stress, part, material, x_first, x_second,
    own_right, own_left, y_first, y_second, stress_out, veloc_out, charge,
    new_stress, new_veloc, sems,
):
    leaving = copies([(new_stress, stress_out), (new_veloc, veloc_out)], sems)
    lane = lax.broadcasted_iota(jnp.int32, (BX, BY), 1)
    corner_lane = lane[:NZ]
    row8 = lax.broadcasted_iota(jnp.int32, (8, BY), 0)
    low, high = low_high("gx", x_first, x_second)
    y_odd = odd("gy")
    from_left = jnp.where(y_odd, y_first[...], y_second[...])
    from_right = jnp.where(y_odd, y_second[...], y_first[...])
    west, east = from_left[:BX], from_right[:BX]
    mine_east, mine_west = own_right[...], own_left[...]

    def shifted(values, by):
        return pltpu.roll(values, (-by * NZ) % BY, 1)

    uy_west = west + shifted(west, 1) * shifted(mine_west, 3)
    ux_east = east - shifted(east, 2) * shifted(mine_east, 2)
    uz_east = shifted(east, 1) - shifted(east, 2) * shifted(mine_east, 3)
    west_corner, east_corner = from_left[BX:], from_right[BX:]
    ux_low = low[0] - jnp.where(corner_lane == 0, low[1] * west_corner[:, 0:1], 0.0)
    uy_high = high[0] + jnp.where(corner_lane == BY - 1, high[2] * east_corner[:, 0:1], 0.0)
    uz_high = high[1] - jnp.where(corner_lane == 0, high[2] * west_corner[:, 1:2], 0.0)

    def beside(values, spot):
        return jnp.broadcast_to(values[:, spot : spot + 1], (BX, BY))

    def at_top(values, added):
        head = values[:8] + jnp.where(row8 == 0, added, 0.0)
        return jnp.concatenate([head, values[8:]], axis=0)

    def at_end(values, added):
        tail = values[BX - 8 :] + jnp.where(row8 == 7, added, 0.0)
        return jnp.concatenate([values[: BX - 8], tail], axis=0)

    def close_edges(z):
        b = pick(material[z], buoy)
        row = slice(z, z + 1)
        head, tail = b[:8], b[BX - 8 :]
        ux = part[0, z] - jnp.where(lane == 0, b * beside(west, 2 * NZ + z), 0.0)
        uy = part[1, z] + jnp.where(lane == BY - 1, b * beside(east, 3 * NZ + z), 0.0)
        uz = part[2, z] - jnp.where(lane == 0, b * beside(west, 3 * NZ + z), 0.0)
        new_veloc[0, z] = at_end(ux, tail * high[3][row])
        new_veloc[1, z] = at_top(uy, -(head * low[2][row]))
        new_veloc[2, z] = at_top(uz, -(head * low[3][row]))

    for step in range(NZ + 1):
        if step < NZ:
            close_edges(step)
        if step == 0:
            continue
        z = step - 1
        sxx, syy, szz, sxy, sxz, syz = (stress[c, z] for c in range(6))
        ux, uy, uz = (new_veloc[c, z] for c in range(3))
        codes = material[z]
        lam, mu, e = pick(codes, lame), pick(codes, shear), pick(codes, piezo)
        row = slice(z, z + 1)
        ex = ux - last_row(ux, ux_low[row] + low[1][row] * sxx[0:1])
        ey = uy - jnp.where(lane == 0, beside(uy_west, z), pltpu.roll(uy, 1, 1))
        ez = uz - new_veloc[2, z - 1] if z else uz
        lam_div = lam * (ex + ey + ez)
        mu2 = 2.0 * mu
        new_stress[0, z] = sxx + lam_div + mu2 * ex
        new_stress[1, z] = syy + lam_div + mu2 * ey
        new_stress[2, z] = szz + lam_div + mu2 * ez
        b_high = high[2][row]
        dx_uy = next_row(uy, uy_high[row] - b_high * sxy[BX - 1 : BX]) - uy
        dx_uz = next_row(uz, uz_high[row] - b_high * sxz[BX - 1 : BX]) - uz
        last = lane == BY - 1
        dy_ux = jnp.where(last, beside(ux_east, z), pltpu.roll(ux, BY - 1, 1)) - ux
        dy_uz = jnp.where(last, beside(uz_east, z), pltpu.roll(uz, BY - 1, 1)) - uz
        dz_ux = new_veloc[0, z + 1] - ux if z < NZ - 1 else -ux
        dz_uy = new_veloc[1, z + 1] - uy if z < NZ - 1 else -uy
        new_sxz = sxz + mu * (dz_ux + dx_uz)
        new_syz = syz + mu * (dz_uy + dy_uz)
        new_stress[3, z] = sxy + mu * (dy_ux + dx_uy)
        new_stress[4, z] = new_sxz
        new_stress[5, z] = new_syz
        charge[z] = e * (new_sxz + new_syz)
        if z % CHUNK == CHUNK - 1:
            for copy in leaving[z // CHUNK]:
                copy.start()
    for chunk in leaving:
        for copy in chunk:
            copy.wait()


ROOT = math.sqrt(0.5)


def real_dft8(c):
    s = [c[i] + c[i + 4] for i in range(4)]
    d = [c[i] - c[i + 4] for i in range(4)]
    even, odd = s[0] + s[2], s[1] + s[3]
    near, far = ROOT * (d[1] - d[3]), ROOT * (d[1] + d[3])
    re1, re3 = d[0] + near, d[0] - near
    im1, im3 = -(d[2] + far), d[2] - far
    re2, im2 = s[0] - s[2], s[3] - s[1]
    zero = None
    return [
        (even + odd, zero), (re1, im1), (re2, im2), (re3, im3),
        (even - odd, zero), (re3, -im3), (re2, -im2), (re1, -im1),
    ]


def transform_y(charge, w_high, w_low, twiddle, out, real_lines, imag_lines):
    for z in range(2):
        for ihi in range(4):
            at = slice(16 * ihi, 16 * ihi + 16)
            modes = real_dft8([charge[g, z, at, :] for g in range(8)])
            for a, (re, im) in enumerate(modes):
                cos, sin = twiddle[2 * a : 2 * a + 1, :], twiddle[2 * a + 1 : 2 * a + 2, :]
                if a == 0:
                    new_re, new_im = re, jnp.zeros_like(re)
                elif im is None:
                    new_re, new_im = re * cos, -(re * sin)
                else:
                    new_re, new_im = re * cos + im * sin, im * cos - re * sin
                base = (ihi * 2 + a // 4) * 128 + z * 4 + a % 4
                real_lines[pl.ds(base, 16, stride=8), :] = new_re
                imag_lines[pl.ds(base, 16, stride=8), :] = new_im
    weights = (w_high[...], w_low[...])
    for ihi in range(4):
        for ahi in range(2):
            block = slice((ihi * 2 + ahi) * 128, (ihi * 2 + ahi + 1) * 128)
            lines = jnp.concatenate([real_lines[block, :], imag_lines[block, :]], axis=1)
            modes = dot3(weights, split(lines), ((1,), (1,)))
            for part in range(2):
                start = ahi * 8 + part * 4 + ihi
                out[pl.ds(start, 128, stride=16), :] = modes[part * 128 : (part + 1) * 128]


def butterfly4(x):
    (ar, ai), (br, bi) = (
        (x[0][0] + x[2][0], x[0][1] + x[2][1]),
        (x[0][0] - x[2][0], x[0][1] - x[2][1]),
    )
    (cr, ci), (dr, di) = (
        (x[1][0] + x[3][0], x[1][1] + x[3][1]),
        (x[1][0] - x[3][0], x[1][1] - x[3][1]),
    )
    return [(ar + cr, ai + ci), (br + di, bi - dr), (ar - cr, ai - ci), (br - di, bi + dr)]


def turned(value, step):
    re, im = value
    step %= 16
    if step == 0:
        return value
    if step == 4:
        return im, -re
    if step == 2:
        return ROOT * (re + im), ROOT * (im - re)
    if step == 6:
        return ROOT * (im - re), -ROOT * (re + im)
    cos, sin = math.cos(2 * math.pi * step / 16), math.sin(2 * math.pi * step / 16)
    return re * cos + im * sin, im * cos - re * sin


def dft16(x):
    inner = [butterfly4([x[4 * na + nb] for na in range(4)]) for nb in range(4)]
    result = [None] * 16
    for ka in range(4):
        outer = butterfly4([turned(inner[nb][ka], nb * ka) for nb in range(4)])
        for kb in range(4):
            result[ka + 4 * kb] = outer[kb]
    return result


def coupling_scalars(layer_kind, lateral, normal):
    def at(table, kind):
        return jnp.where(kind == 0, table[0], jnp.where(kind == 1, table[1], table[2]))

    el = [at(lateral, layer_kind[z]) for z in range(NZ)]
    en = [at(normal, layer_kind[z]) for z in range(NZ)]
    g = [en[0]] + [0.5 * (en[z - 1] + en[z]) for z in range(1, NZ)] + [en[-1]]
    return el, g


def pivots(layer_kind, lateral, normal, wave_x, inverse):
    el, g = coupling_scalars(layer_kind, lateral, normal)
    first = (lax.axis_index("gx") * DY + lax.axis_index("gy")) * 4
    ky = first + rows(jnp.zeros((8, 128), jnp.float32)) % 4
    wave_y = 2.0 * jnp.sin(math.pi * ky.astype(jnp.float32) / NY)
    wave_y = wave_y * wave_y
    for k in range(NX // 512):
        at = slice(512 * k, 512 * k + 512)
        wave = jnp.concatenate([wave_y] * 4, axis=1) + wave_x[:, at]
        factor = None
        for z in range(NZ):
            pivot = g[z] + g[z + 1] + wave * el[z]
            if z:
                pivot = pivot - g[z] * factor
            inv = 1.0 / pivot
            inverse[z, :, at] = inv
            factor = g[z + 1] * inv


SPAN = 512


def solve(
    layer_kind, lateral, normal, lines, w_high, w_low, twiddle, inverse, modes_out, rhs, out, sems
):
    weights = (w_high[...], w_low[...])
    upper = rows(jnp.zeros((8, 128), jnp.float32)) < 4
    for gy in range(DY):
        block = lines[:, gy].reshape(256, 128)
        modes = dot3(split(block.T), weights, ((1,), (0,)))
        turned_modes = []
        for n2 in range(16):
            re, im = modes[8 * n2 : 8 * n2 + 8, :128], modes[8 * n2 : 8 * n2 + 8, 128:]
            if n2:
                cos, sin = twiddle[2 * n2 : 2 * n2 + 1, :], twiddle[2 * n2 + 1 : 2 * n2 + 2, :]
                re, im = re * cos + im * sin, im * cos - re * sin
            turned_modes.append((re, im))
        for k2, (re, im) in enumerate(dft16(turned_modes)):
            at = slice(128 * k2, 128 * k2 + 128)
            rhs[2 * gy, :, at] = jnp.where(upper, re, pltpu.roll(im, 4, 0))
            rhs[2 * gy + 1, :, at] = jnp.where(upper, pltpu.roll(re, 4, 0), im)
    _, g = coupling_scalars(layer_kind, lateral, normal)
    leaving = []
    for k in range(NX // 256):
        at = slice(256 * k, 256 * k + 256)
        sums = []
        for z in range(NZ):
            value = rhs[z, :, at]
            if z:
                value = value + g[z] * (sums[-1] * inverse[z - 1, :, at])
            sums.append(value)
        above = None
        for z in range(NZ - 1, -1, -1):
            value = sums[z]
            if above is not None:
                value = value + g[z + 1] * above
            above = value * inverse[z, :, at]
            out[0, z, :, at] = above[:4]
            out[1, z, :, at] = above[4:]
        if (k + 1) * 256 % SPAN == 0:
            done = pl.ds((k + 1) * 256 - SPAN, SPAN)
            leaving.append(
                pltpu.make_async_copy(
                    out.at[:, :, :, done], modes_out.at[:, :, :, done], sems.at[len(leaving)]
                )
            )
            leaving[-1].start()
    for copy in leaving:
        copy.wait()


SMEM = pl.BlockSpec(memory_space=pltpu.SMEM)
VMEM = pl.BlockSpec(memory_space=pltpu.VMEM)
ANY = pl.BlockSpec(memory_space=pl.ANY)


def near(*values):
    return tuple(pltpu.with_memory_space_constraint(value, pltpu.VMEM) for value in values)


def call(body, name, outs, in_specs, args, scratch=(), out_specs=None, flops=1_000_000, keep=()):
    shapes = [
        pltpu.VMEM(shape, jnp.float32) if n in keep else jax.ShapeDtypeStruct(shape, jnp.float32)
        for n, shape in enumerate(outs)
    ]
    moved = sum(4 * math.prod(shape) for shape in outs) + sum(4 * v.size for v in args)
    return pl.pallas_call(
        body,
        name=name,
        out_shape=shapes,
        in_specs=in_specs,
        out_specs=out_specs or [VMEM] * len(outs),
        scratch_shapes=list(scratch),
        compiler_params=pltpu.CompilerParams(vmem_limit_bytes=KEPT_LIMIT),
        cost_estimate=pl.CostEstimate(flops=flops, bytes_accessed=moved, transcendentals=0),
    )(*args)


def field(count, dtype=jnp.float32):
    shape = (NZ, BX, BY)
    return pltpu.VMEM(shape if count == 1 else (count, *shape), dtype)


def swaps(axis, first, second):
    def pairs(start):
        both = [(i, i + 1) for i in range(start, lax.axis_size(axis) - 1, 2)]
        return both + [(b, a) for a, b in both]

    second = lax.ppermute(second, axis, pairs(1))
    return lax.ppermute(first, axis, pairs(0)), second


def per_device(
    stress, velocity, material, layer_kind, buoyancy, lame_first, shear_modulus, piezo, permit_lateral, permit_normal
):
    x_edges = call(
        edge_rows,
        "edge_rows",
        [(6, NZ, BY)] * 2,
        [SMEM] + [ANY] * 3,
        (buoyancy, *(pltpu.with_memory_space_constraint(v, pltpu.HBM) for v in (stress, velocity, material))),
        [
            pltpu.VMEM((2, 6, NZ, 1, BY), jnp.float32),
            pltpu.VMEM((2, 3, NZ, 1, BY), jnp.float32),
            pltpu.VMEM((2, NZ, 1, BY), jnp.int32),
            pltpu.SemaphoreType.DMA((2, 3)),
        ],
        keep=(0, 1),
    )
    x_edges = near(*swaps("gx", *x_edges))
    stress, velocity, material = near(stress, velocity, material)
    part, own_right, own_left = call(
        advance_velocity,
        "advance_velocity",
        [(3, NZ, BX, BY), (BX, BY), (BX, BY)],
        [SMEM] + [VMEM] * 3,
        (buoyancy, stress, velocity, material),
        keep=(0, 1, 2),
    )
    scalars = (layer_kind, permit_lateral, permit_normal)
    own_right, layer_kind = lax.optimization_barrier((own_right, layer_kind))
    inverse, = call(
        pivots,
        "pivots",
        [(NZ, 8, NX)],
        [SMEM] * 3 + [VMEM],
        (layer_kind, permit_lateral, permit_normal, jnp.asarray(table_wave())),
        keep=(0,),
    )
    own_right, inverse = lax.optimization_barrier((own_right, inverse))
    own_right, inverse = near(own_right, inverse)
    y_edges = call(
        edge_columns,
        "edge_columns",
        [(BX + NZ, BY)] * 2,
        [VMEM] * 4,
        (own_right, own_left, *x_edges),
        keep=(0, 1),
    )
    y_edges = near(*swaps("gy", *y_edges))
    stress_next, velocity_next, charge = call(
        advance_stress,
        "advance_stress",
        [(6, NZ, BX, BY), (3, NZ, BX, BY), (NZ, BX, BY)],
        [SMEM] * 4 + [VMEM] * 9,
        (
            buoyancy, lame_first, shear_modulus, piezo, stress, part, material,
            *x_edges, own_right, own_left, *y_edges,
        ),
        [field(6), field(3), pltpu.SemaphoreType.DMA((NZ // CHUNK, 2))],
        [ANY, ANY, VMEM],
        keep=(2,),
    )
    charge = lax.all_to_all(charge, "gy", 0, 0, tiled=True).reshape(DY, 2, BX, BY)
    modes, = call(
        transform_y,
        "transform_y",
        [(NY * 2, 128)],
        [VMEM] * 4,
        (*near(charge), *(jnp.asarray(t) for t in tables_y())),
        [pltpu.VMEM((1024, 128), jnp.float32)] * 2,
        keep=(0,),
    )
    lines = lax.all_to_all(modes.reshape(DX * DY, 8, 128), ("gx", "gy"), 0, 0, tiled=True)
    potential_modes, = call(
        solve,
        "solve",
        [(2, NZ, 4, NX)],
        [SMEM] * 3 + [VMEM] * 5,
        (*scalars, *near(lines.reshape(DX, DY, 8, 128)), *(jnp.asarray(t) for t in tables_x()), inverse),
        [
            pltpu.VMEM((NZ, 8, NX), jnp.float32),
            pltpu.VMEM((2, NZ, 4, NX), jnp.float32),
            pltpu.SemaphoreType.DMA((NX // SPAN,)),
        ],
        [ANY],
    )
    return (stress_next, velocity_next, potential_modes)


def solution(mesh):
    spread = P(None, None, "gx", "gy")
    return jax.shard_map(
        per_device,
        mesh=mesh,
        in_specs=(spread, spread, P(None, "gx", "gy")) + (P(),) * 7,
        out_specs=(spread, spread, P(None, None, ("gx", "gy"), None)),
        check_vma=False,
    )
```

```python
import functools
import math

import jax
import jax.numpy as jnp
import ml_dtypes
import numpy as np
from jax import lax
from jax.experimental import pallas as pl
from jax.experimental.pallas import tpu as pltpu
from jax.sharding import PartitionSpec as P

NZ = 16
NX = 2048
NY = 1024
DX = 32
DY = 8
BX = NX // DX
BY = NY // DY
KEPT_LIMIT = 24 * 1024 * 1024


def halves(values):
    high = values.astype(ml_dtypes.bfloat16)
    low = (values - high.astype(np.float64)).astype(ml_dtypes.bfloat16)
    return high, low


def split(values):
    high = values.astype(jnp.bfloat16)
    low = (values - high.astype(jnp.float32)).astype(jnp.bfloat16)
    return high, low


def tables_y():
    j = np.arange(128)
    a = np.arange(8)
    angle = 2.0 * np.pi * (np.outer(j, j) % 128) / 128
    cos, sin = np.cos(angle) / 32.0, np.sin(angle) / 32.0
    weights = np.block([[cos, sin], [-sin, cos]])
    turn = 2.0 * np.pi * np.outer(a, j) / NY
    twiddle = np.stack([np.cos(turn), np.sin(turn)], axis=1).reshape(16, 128)
    return *halves(weights), twiddle.astype(np.float32)


def tables_x():
    n1 = np.arange(128)
    angle = 2.0 * np.pi * (np.outer(n1, n1) % 128) / 128
    scale = 1.0 / math.sqrt(NX)
    cos, sin = np.cos(angle) * scale, np.sin(angle) * scale
    real_rows = np.concatenate([cos, -sin], axis=1).reshape(DX, 1, 4, 256)
    imag_rows = np.concatenate([sin, cos], axis=1).reshape(DX, 1, 4, 256)
    weights = np.concatenate([real_rows, imag_rows], axis=1).reshape(256, 256)
    turn = 2.0 * np.pi * np.outer(np.arange(16), n1) / NX
    twiddle = np.stack([np.cos(turn), np.sin(turn)], axis=1).reshape(32, 128)
    return *halves(weights), twiddle.astype(np.float32)


def table_wave():
    wave = 2.0 * np.sin(np.pi * np.arange(NX) / NX)
    return (wave * wave).astype(np.float32).reshape(1, NX)


def dot3(a, b, dims):
    (a_high, a_low), (b_high, b_low) = a, b
    dot = functools.partial(
        lax.dot_general, dimension_numbers=(dims, ((), ())), preferred_element_type=jnp.float32
    )
    return dot(a_high, b_high) + (dot(a_low, b_high) + dot(a_high, b_low))


def pick(codes, table_ref):
    first, second, third = table_ref[0], table_ref[1], table_ref[2]
    return jnp.where(codes == 0, first, jnp.where(codes == 1, second, third))


def lanes(values):
    return lax.broadcasted_iota(jnp.int32, values.shape, values.ndim - 1)


def rows(values):
    return lax.broadcasted_iota(jnp.int32, values.shape, values.ndim - 2)


def next_lane(values):
    moved = pltpu.roll(values, values.shape[-1] - 1, values.ndim - 1)
    return jnp.where(lanes(values) == values.shape[-1] - 1, 0.0, moved)


def last_lane(values):
    moved = pltpu.roll(values, 1, values.ndim - 1)
    return jnp.where(lanes(values) == 0, 0.0, moved)


def next_row(values, edge):
    size = values.shape[0]
    moved = pltpu.roll(values, size - 1, 0)
    tail = moved[size - 8 :]
    tail = jnp.where(rows(tail) == 7, edge, tail)
    return jnp.concatenate([moved[: size - 8], tail], axis=0)


def last_row(values, edge):
    moved = pltpu.roll(values, 1, 0)
    head = jnp.where(rows(moved[:8]) == 0, edge, moved[:8])
    return jnp.concatenate([head, moved[8:]], axis=0)


def next_layer(values):
    size = values.shape[0]
    moved = pltpu.roll(values, size - 1, 0)
    return jnp.where(rows(values) == size - 1, 0.0, moved)


def last_layer(values):
    moved = pltpu.roll(values, 1, 0)
    return jnp.where(rows(values) == 0, 0.0, moved)


def odd(axis):
    return lax.axis_index(axis) % 2 == 1


def low_high(axis, first, second):
    is_odd = odd(axis)
    low = [jnp.where(is_odd, first[c], second[c]) for c in range(first.shape[0])]
    high = [jnp.where(is_odd, second[c], first[c]) for c in range(first.shape[0])]
    return low, high


def edge_rows(
    buoy_in, stress_in, veloc_in, material_in, second, first, stress, veloc, material, buoy, sems, buoy_sem
):
    moves = [pltpu.make_async_copy(buoy_in, buoy, buoy_sem)]
    for n, row in enumerate((0, BX - 1)):
        at = pl.ds(row, 1)
        moves += [
            pltpu.make_async_copy(stress_in.at[:, :, at], stress.at[n], sems.at[n, 0]),
            pltpu.make_async_copy(veloc_in.at[:, :, at], veloc.at[n], sems.at[n, 1]),
            pltpu.make_async_copy(material_in.at[:, at], material.at[n], sems.at[n, 2]),
        ]
    for move in moves:
        move.start()
    for move in moves:
        move.wait()
    sxx, sxy, sxz = (stress[1, c, :, 0, :] for c in (0, 3, 4))
    b = pick(material[1, :, 0, :], buoy)
    ux = veloc[1, 0, :, 0, :] + b * ((sxy - last_lane(sxy)) + (sxz - last_layer(sxz)) - sxx)
    down = [ux, b, sxy, sxz, jnp.zeros_like(b), jnp.zeros_like(b)]
    sxx, syy, szz, sxy, sxz, syz = (stress[0, c, :, 0, :] for c in range(6))
    b = pick(material[0, :, 0, :], buoy)
    uy = veloc[0, 1, :, 0, :] + b * (sxy + (next_lane(syy) - syy) + (syz - last_layer(syz)))
    uz = veloc[0, 2, :, 0, :] + b * (sxz + (syz - last_lane(syz)) + (next_layer(szz) - szz))
    up = [uy, uz, b, sxx, syy, syz]
    is_odd = odd("gx")
    for c in range(6):
        first[c] = jnp.where(is_odd, up[c], down[c])
        second[c] = jnp.where(is_odd, down[c], up[c])


CHUNK = 2


def copies(pairs, sems):
    made = []
    for k in range(NZ // CHUNK):
        at = pl.ds(k * CHUNK, CHUNK)
        made.append([])
        for n, (source, target) in enumerate(pairs):
            index = (at,) if len(source.shape) == 3 else (slice(None), at)
            made[-1].append(pltpu.make_async_copy(source.at[index], target.at[index], sems.at[k, n]))
    return made


def advance_velocity(buoy, stress, veloc, material, new, right_ref, left_ref):
    column = lax.broadcasted_iota(jnp.int32, (BX, BY), 1)
    right = jnp.zeros((BX, BY), jnp.float32)
    left = jnp.zeros((BX, BY), jnp.float32)
    for z in range(NZ):
        sxx, syy, szz, sxy, sxz, syz = (stress[c, z] for c in range(6))
        b = pick(material[z], buoy)
        dz_sxz = sxz - stress[4, z - 1] if z else sxz
        dz_syz = syz - stress[5, z - 1] if z else syz
        dz_szz = stress[2, z + 1] - szz if z < NZ - 1 else -szz
        ux = veloc[0, z] + b * ((next_row(sxx, 0.0) - sxx) + (sxy - last_lane(sxy)) + dz_sxz)
        uy = veloc[1, z] + b * ((sxy - last_row(sxy, 0.0)) + (next_lane(syy) - syy) + dz_syz)
        uz = veloc[2, z] + b * ((sxz - last_row(sxz, 0.0)) + (syz - last_lane(syz)) + dz_szz)
        new[0, z] = ux
        new[1, z] = uy
        new[2, z] = uz
        for part, value in enumerate((uy, b, sxy, syz)):
            spot = part * NZ + z
            moved = pltpu.roll(value, (spot + 1) % BY, 1)
            right = jnp.where(column == spot, moved, right)
        for part, value in enumerate((ux, uz, b, syy)):
            spot = part * NZ + z
            moved = pltpu.roll(value, spot, 1) if spot else value
            left = jnp.where(column == spot, moved, left)
    right_ref[...] = right
    left_ref[...] = left


def edge_columns(right_ref, left_ref, x_second, x_first, second, first):
    low, high = low_high("gx", x_first, x_second)
    corner = lax.broadcasted_iota(jnp.int32, (NZ, BY), 1)
    layer = lax.broadcasted_iota(jnp.int32, (NZ, BY), 0)
    row = lax.broadcasted_iota(jnp.int32, (BX, BY), 0)
    column = lax.broadcasted_iota(jnp.int32, (BX, BY), 1)

    def line(values, spot, at):
        wide = jnp.broadcast_to(values[:, spot : spot + 1], (NZ, BY))
        return jnp.sum(jnp.where(corner == layer + at, wide, 0.0), axis=0, keepdims=True)

    def shifted(values, by):
        return pltpu.roll(values, (-by * NZ) % BY, 1)

    right, left = right_ref[...], left_ref[...]
    right_b = shifted(right, 1)
    right = right - jnp.where((row == 0) & (column < NZ), right_b * line(low[2], BY - 1, 0), 0.0)
    left_b = jnp.where(column < NZ, shifted(left, 2), shifted(left, 1))
    left = left + jnp.where((row == BX - 1) & (column < NZ), left_b * line(high[3], 0, 0), 0.0)
    left = left - jnp.where(
        (row == 0) & (column >= NZ) & (column < 2 * NZ), left_b * line(low[3], 0, NZ), 0.0
    )
    right_corner = jnp.where(
        corner == 0, pltpu.roll(low[2], 1, 1), jnp.where(corner == 1, pltpu.roll(high[5], 2, 1), 0.0)
    )
    left_corner = jnp.where(corner == 0, high[4], 0.0)
    is_odd = odd("gy")
    first[:BX] = jnp.where(is_odd, left, right)
    first[BX:] = jnp.where(is_odd, left_corner, right_corner)
    second[:BX] = jnp.where(is_odd, right, left)
    second[BX:] = jnp.where(is_odd, right_corner, left_corner)


def advance_stress(
    buoy, lame, shear, piezo, stress, part, material, x_second, x_first,
    own_right, own_left, y_second, y_first, stress_out, veloc_out, charge,
    new_stress, new_veloc, sems,
):
    leaving = copies([(new_stress, stress_out), (new_veloc, veloc_out)], sems)
    lane = lax.broadcasted_iota(jnp.int32, (BX, BY), 1)
    corner_lane = lane[:NZ]
    row8 = lax.broadcasted_iota(jnp.int32, (8, BY), 0)
    low, high = low_high("gx", x_first, x_second)
    y_odd = odd("gy")
    from_left = jnp.where(y_odd, y_first[...], y_second[...])
    from_right = jnp.where(y_odd, y_second[...], y_first[...])
    west, east = from_left[:BX], from_right[:BX]
    mine_east, mine_west = own_right[...], own_left[...]

    def shifted(values, by):
        return pltpu.roll(values, (-by * NZ) % BY, 1)

    uy_west = west + shifted(west, 1) * shifted(mine_west, 3)
    ux_east = east - shifted(east, 2) * shifted(mine_east, 2)
    uz_east = shifted(east, 1) - shifted(east, 2) * shifted(mine_east, 3)
    west_corner, east_corner = from_left[BX:], from_right[BX:]
    ux_low = low[0] - jnp.where(corner_lane == 0, low[1] * west_corner[:, 0:1], 0.0)
    uy_high = high[0] + jnp.where(corner_lane == BY - 1, high[2] * east_corner[:, 0:1], 0.0)
    uz_high = high[1] - jnp.where(corner_lane == 0, high[2] * west_corner[:, 1:2], 0.0)

    def beside(values, spot):
        return jnp.broadcast_to(values[:, spot : spot + 1], (BX, BY))

    def at_top(values, added):
        head = values[:8] + jnp.where(row8 == 0, added, 0.0)
        return jnp.concatenate([head, values[8:]], axis=0)

    def at_end(values, added):
        tail = values[BX - 8 :] + jnp.where(row8 == 7, added, 0.0)
        return jnp.concatenate([values[: BX - 8], tail], axis=0)

    def close_edges(z):
        b = pick(material[z], buoy)
        row = slice(z, z + 1)
        head, tail = b[:8], b[BX - 8 :]
        ux = part[0, z] - jnp.where(lane == 0, b * beside(west, 2 * NZ + z), 0.0)
        uy = part[1, z] + jnp.where(lane == BY - 1, b * beside(east, 3 * NZ + z), 0.0)
        uz = part[2, z] - jnp.where(lane == 0, b * beside(west, 3 * NZ + z), 0.0)
        new_veloc[0, z] = at_end(ux, tail * high[3][row])
        new_veloc[1, z] = at_top(uy, -(head * low[2][row]))
        new_veloc[2, z] = at_top(uz, -(head * low[3][row]))

    for step in range(NZ + 1):
        if step < NZ:
            close_edges(step)
        if step == 0:
            continue
        z = step - 1
        sxx, syy, szz, sxy, sxz, syz = (stress[c, z] for c in range(6))
        ux, uy, uz = (new_veloc[c, z] for c in range(3))
        codes = material[z]
        lam, mu, e = pick(codes, lame), pick(codes, shear), pick(codes, piezo)
        row = slice(z, z + 1)
        ex = ux - last_row(ux, ux_low[row] + low[1][row] * sxx[0:1])
        ey = uy - jnp.where(lane == 0, beside(uy_west, z), pltpu.roll(uy, 1, 1))
        ez = uz - new_veloc[2, z - 1] if z else uz
        lam_div = lam * (ex + ey + ez)
        mu2 = 2.0 * mu
        new_stress[0, z] = sxx + lam_div + mu2 * ex
        new_stress[1, z] = syy + lam_div + mu2 * ey
        new_stress[2, z] = szz + lam_div + mu2 * ez
        b_high = high[2][row]
        dx_uy = next_row(uy, uy_high[row] - b_high * sxy[BX - 1 : BX]) - uy
        dx_uz = next_row(uz, uz_high[row] - b_high * sxz[BX - 1 : BX]) - uz
        last = lane == BY - 1
        dy_ux = jnp.where(last, beside(ux_east, z), pltpu.roll(ux, BY - 1, 1)) - ux
        dy_uz = jnp.where(last, beside(uz_east, z), pltpu.roll(uz, BY - 1, 1)) - uz
        dz_ux = new_veloc[0, z + 1] - ux if z < NZ - 1 else -ux
        dz_uy = new_veloc[1, z + 1] - uy if z < NZ - 1 else -uy
        new_sxz = sxz + mu * (dz_ux + dx_uz)
        new_syz = syz + mu * (dz_uy + dy_uz)
        new_stress[3, z] = sxy + mu * (dy_ux + dx_uy)
        new_stress[4, z] = new_sxz
        new_stress[5, z] = new_syz
        charge[z] = e * (new_sxz + new_syz)
        if z % CHUNK == CHUNK - 1:
            for copy in leaving[z // CHUNK]:
                copy.start()
    for chunk in leaving:
        for copy in chunk:
            copy.wait()


ROOT = math.sqrt(0.5)


def real_dft8(c):
    s = [c[i] + c[i + 4] for i in range(4)]
    d = [c[i] - c[i + 4] for i in range(4)]
    even, odd = s[0] + s[2], s[1] + s[3]
    near, far = ROOT * (d[1] - d[3]), ROOT * (d[1] + d[3])
    re1, re3 = d[0] + near, d[0] - near
    im1, im3 = -(d[2] + far), d[2] - far
    re2, im2 = s[0] - s[2], s[3] - s[1]
    zero = None
    return [
        (even + odd, zero), (re1, im1), (re2, im2), (re3, im3),
        (even - odd, zero), (re3, -im3), (re2, -im2), (re1, -im1),
    ]


def transform_y(charge, w_high, w_low, twiddle, out, real_lines, imag_lines):
    for z in range(2):
        for ihi in range(4):
            at = slice(16 * ihi, 16 * ihi + 16)
            modes = real_dft8([charge[g, z, at, :] for g in range(8)])
            for a, (re, im) in enumerate(modes):
                cos, sin = twiddle[2 * a : 2 * a + 1, :], twiddle[2 * a + 1 : 2 * a + 2, :]
                if a == 0:
                    new_re, new_im = re, jnp.zeros_like(re)
                elif im is None:
                    new_re, new_im = re * cos, -(re * sin)
                else:
                    new_re, new_im = re * cos + im * sin, im * cos - re * sin
                base = (ihi * 2 + a // 4) * 128 + z * 4 + a % 4
                real_lines[pl.ds(base, 16, stride=8), :] = new_re
                imag_lines[pl.ds(base, 16, stride=8), :] = new_im
    weights = (w_high[...], w_low[...])
    for ihi in range(4):
        for ahi in range(2):
            block = slice((ihi * 2 + ahi) * 128, (ihi * 2 + ahi + 1) * 128)
            lines = jnp.concatenate([real_lines[block, :], imag_lines[block, :]], axis=1)
            modes = dot3(weights, split(lines), ((1,), (1,)))
            for part in range(2):
                start = ahi * 8 + part * 4 + ihi
                out[pl.ds(start, 128, stride=16), :] = modes[part * 128 : (part + 1) * 128]


def butterfly4(x):
    (ar, ai), (br, bi) = (
        (x[0][0] + x[2][0], x[0][1] + x[2][1]),
        (x[0][0] - x[2][0], x[0][1] - x[2][1]),
    )
    (cr, ci), (dr, di) = (
        (x[1][0] + x[3][0], x[1][1] + x[3][1]),
        (x[1][0] - x[3][0], x[1][1] - x[3][1]),
    )
    return [(ar + cr, ai + ci), (br + di, bi - dr), (ar - cr, ai - ci), (br - di, bi + dr)]


def turned(value, step):
    re, im = value
    step %= 16
    if step == 0:
        return value
    if step == 4:
        return im, -re
    if step == 2:
        return ROOT * (re + im), ROOT * (im - re)
    if step == 6:
        return ROOT * (im - re), -ROOT * (re + im)
    cos, sin = math.cos(2 * math.pi * step / 16), math.sin(2 * math.pi * step / 16)
    return re * cos + im * sin, im * cos - re * sin


def dft16(x):
    inner = [butterfly4([x[4 * na + nb] for na in range(4)]) for nb in range(4)]
    result = [None] * 16
    for ka in range(4):
        outer = butterfly4([turned(inner[nb][ka], nb * ka) for nb in range(4)])
        for kb in range(4):
            result[ka + 4 * kb] = outer[kb]
    return result


def coupling_scalars(layer_kind, lateral, normal):
    def at(table, kind):
        return jnp.where(kind == 0, table[0], jnp.where(kind == 1, table[1], table[2]))

    el = [at(lateral, layer_kind[z]) for z in range(NZ)]
    en = [at(normal, layer_kind[z]) for z in range(NZ)]
    g = [en[0]] + [0.5 * (en[z - 1] + en[z]) for z in range(1, NZ)] + [en[-1]]
    return el, g


def pivots(layer_kind, lateral, normal, wave_x, inverse):
    el, g = coupling_scalars(layer_kind, lateral, normal)
    first = (lax.axis_index("gx") * DY + lax.axis_index("gy")) * 4
    ky = first + rows(jnp.zeros((8, 128), jnp.float32)) % 4
    wave_y = 2.0 * jnp.sin(math.pi * ky.astype(jnp.float32) / NY)
    wave_y = wave_y * wave_y
    for k in range(NX // 512):
        at = slice(512 * k, 512 * k + 512)
        wave = jnp.concatenate([wave_y] * 4, axis=1) + wave_x[:, at]
        factor = None
        for z in range(NZ):
            pivot = g[z] + g[z + 1] + wave * el[z]
            if z:
                pivot = pivot - g[z] * factor
            inv = 1.0 / pivot
            inverse[z, :, at] = inv
            factor = g[z + 1] * inv


SPAN = 512


def solve(
    layer_kind, lateral, normal, lines, w_high, w_low, twiddle, inverse, modes_out, rhs, out, sems
):
    weights = (w_high[...], w_low[...])
    upper = rows(jnp.zeros((8, 128), jnp.float32)) < 4
    for gy in range(DY):
        block = lines[:, gy].reshape(256, 128)
        modes = dot3(split(block.T), weights, ((1,), (0,)))
        turned_modes = []
        for n2 in range(16):
            re, im = modes[8 * n2 : 8 * n2 + 8, :128], modes[8 * n2 : 8 * n2 + 8, 128:]
            if n2:
                cos, sin = twiddle[2 * n2 : 2 * n2 + 1, :], twiddle[2 * n2 + 1 : 2 * n2 + 2, :]
                re, im = re * cos + im * sin, im * cos - re * sin
            turned_modes.append((re, im))
        for k2, (re, im) in enumerate(dft16(turned_modes)):
            at = slice(128 * k2, 128 * k2 + 128)
            rhs[2 * gy, :, at] = jnp.where(upper, re, pltpu.roll(im, 4, 0))
            rhs[2 * gy + 1, :, at] = jnp.where(upper, pltpu.roll(re, 4, 0), im)
    _, g = coupling_scalars(layer_kind, lateral, normal)
    leaving = []
    for k in range(NX // 256):
        at = slice(256 * k, 256 * k + 256)
        sums = []
        for z in range(NZ):
            value = rhs[z, :, at]
            if z:
                value = value + g[z] * (sums[-1] * inverse[z - 1, :, at])
            sums.append(value)
        above = None
        for z in range(NZ - 1, -1, -1):
            value = sums[z]
            if above is not None:
                value = value + g[z + 1] * above
            above = value * inverse[z, :, at]
            out[0, z, :, at] = above[:4]
            out[1, z, :, at] = above[4:]
        if (k + 1) * 256 % SPAN == 0:
            done = pl.ds((k + 1) * 256 - SPAN, SPAN)
            leaving.append(
                pltpu.make_async_copy(
                    out.at[:, :, :, done], modes_out.at[:, :, :, done], sems.at[len(leaving)]
                )
            )
            leaving[-1].start()
    for copy in leaving:
        copy.wait()


SMEM = pl.BlockSpec(memory_space=pltpu.SMEM)
VMEM = pl.BlockSpec(memory_space=pltpu.VMEM)
ANY = pl.BlockSpec(memory_space=pl.ANY)


def near(*values):
    return tuple(pltpu.with_memory_space_constraint(value, pltpu.VMEM) for value in values)


def call(body, name, outs, in_specs, args, scratch=(), out_specs=None, flops=1_000_000, keep=()):
    shapes = [
        pltpu.VMEM(shape, jnp.float32) if n in keep else jax.ShapeDtypeStruct(shape, jnp.float32)
        for n, shape in enumerate(outs)
    ]
    moved = sum(4 * math.prod(shape) for shape in outs) + sum(4 * v.size for v in args)
    return pl.pallas_call(
        body,
        name=name,
        out_shape=shapes,
        in_specs=in_specs,
        out_specs=out_specs or [VMEM] * len(outs),
        scratch_shapes=list(scratch),
        compiler_params=pltpu.CompilerParams(vmem_limit_bytes=KEPT_LIMIT),
        cost_estimate=pl.CostEstimate(flops=flops, bytes_accessed=moved, transcendentals=0),
    )(*args)


def field(count, dtype=jnp.float32):
    shape = (NZ, BX, BY)
    return pltpu.VMEM(shape if count == 1 else (count, *shape), dtype)


def swaps(axis, second, first):
    def pairs(start):
        both = [(i, i + 1) for i in range(start, lax.axis_size(axis) - 1, 2)]
        return both + [(b, a) for a, b in both]

    second = lax.ppermute(second, axis, pairs(1))
    return second, lax.ppermute(first, axis, pairs(0))


def per_device(
    stress, velocity, material, layer_kind, buoyancy, lame_first, shear_modulus, piezo, permit_lateral, permit_normal
):
    x_edges = call(
        edge_rows,
        "edge_rows",
        [(6, NZ, BY)] * 2,
        [ANY] * 4,
        tuple(
            pltpu.with_memory_space_constraint(v, pltpu.HBM) for v in (buoyancy, stress, velocity, material)
        ),
        [
            pltpu.VMEM((2, 6, NZ, 1, BY), jnp.float32),
            pltpu.VMEM((2, 3, NZ, 1, BY), jnp.float32),
            pltpu.VMEM((2, NZ, 1, BY), jnp.int32),
            pltpu.SMEM((3,), jnp.float32),
            pltpu.SemaphoreType.DMA((2, 3)),
            pltpu.SemaphoreType.DMA,
        ],
        keep=(0, 1),
    )
    x_edges = near(*swaps("gx", *x_edges))
    stress, velocity, material = near(stress, velocity, material)
    part, own_right, own_left = call(
        advance_velocity,
        "advance_velocity",
        [(3, NZ, BX, BY), (BX, BY), (BX, BY)],
        [SMEM] + [VMEM] * 3,
        (buoyancy, stress, velocity, material),
        keep=(0, 1, 2),
    )
    scalars = (layer_kind, permit_lateral, permit_normal)
    own_right, layer_kind = lax.optimization_barrier((own_right, layer_kind))
    inverse, = call(
        pivots,
        "pivots",
        [(NZ, 8, NX)],
        [SMEM] * 3 + [VMEM],
        (layer_kind, permit_lateral, permit_normal, jnp.asarray(table_wave())),
        keep=(0,),
    )
    own_right, inverse = lax.optimization_barrier((own_right, inverse))
    own_right, inverse = near(own_right, inverse)
    y_edges = call(
        edge_columns,
        "edge_columns",
        [(BX + NZ, BY)] * 2,
        [VMEM] * 4,
        (own_right, own_left, *x_edges),
        keep=(0, 1),
    )
    y_edges = near(*swaps("gy", *y_edges))
    stress_next, velocity_next, charge = call(
        advance_stress,
        "advance_stress",
        [(6, NZ, BX, BY), (3, NZ, BX, BY), (NZ, BX, BY)],
        [SMEM] * 4 + [VMEM] * 9,
        (
            buoyancy, lame_first, shear_modulus, piezo, stress, part, material,
            *x_edges, own_right, own_left, *y_edges,
        ),
        [field(6), field(3), pltpu.SemaphoreType.DMA((NZ // CHUNK, 2))],
        [ANY, ANY, VMEM],
        keep=(2,),
    )
    charge = lax.all_to_all(charge, "gy", 0, 0, tiled=True).reshape(DY, 2, BX, BY)
    modes, = call(
        transform_y,
        "transform_y",
        [(NY * 2, 128)],
        [VMEM] * 4,
        (*near(charge), *(jnp.asarray(t) for t in tables_y())),
        [pltpu.VMEM((1024, 128), jnp.float32)] * 2,
        keep=(0,),
    )
    lines = lax.all_to_all(modes.reshape(DX * DY, 8, 128), ("gx", "gy"), 0, 0, tiled=True)
    potential_modes, = call(
        solve,
        "solve",
        [(2, NZ, 4, NX)],
        [SMEM] * 3 + [VMEM] * 5,
        (*scalars, *near(lines.reshape(DX, DY, 8, 128)), *(jnp.asarray(t) for t in tables_x()), inverse),
        [
            pltpu.VMEM((NZ, 8, NX), jnp.float32),
            pltpu.VMEM((2, NZ, 4, NX), jnp.float32),
            pltpu.SemaphoreType.DMA((NX // SPAN,)),
        ],
        [ANY],
    )
    return (stress_next, velocity_next, potential_modes)


def solution(mesh):
    spread = P(None, None, "gx", "gy")
    return jax.shard_map(
        per_device,
        mesh=mesh,
        in_specs=(spread, spread, P(None, "gx", "gy")) + (P(),) * 7,
        out_specs=(spread, spread, P(None, None, ("gx", "gy"), None)),
        check_vma=False,
    )
```

```python
import functools
import math

import jax
import jax.numpy as jnp
import ml_dtypes
import numpy as np
from jax import lax
from jax.experimental import pallas as pl
from jax.experimental.pallas import tpu as pltpu
from jax.sharding import PartitionSpec as P

NZ = 16
NX = 2048
NY = 1024
DX = 32
DY = 8
BX = NX // DX
BY = NY // DY
KEPT_LIMIT = 24 * 1024 * 1024


def halves(values):
    high = values.astype(ml_dtypes.bfloat16)
    low = (values - high.astype(np.float64)).astype(ml_dtypes.bfloat16)
    return high, low


def split(values):
    high = values.astype(jnp.bfloat16)
    low = (values - high.astype(jnp.float32)).astype(jnp.bfloat16)
    return high, low


def tables_y():
    j = np.arange(128)
    a = np.arange(8)
    angle = 2.0 * np.pi * (np.outer(j, j) % 128) / 128
    cos, sin = np.cos(angle) / 32.0, np.sin(angle) / 32.0
    weights = np.block([[cos, sin], [-sin, cos]])
    turn = 2.0 * np.pi * np.outer(a, j) / NY
    twiddle = np.stack([np.cos(turn), np.sin(turn)], axis=1).reshape(16, 128)
    return *halves(weights), twiddle.astype(np.float32)


def tables_x():
    n1 = np.arange(128)
    angle = 2.0 * np.pi * (np.outer(n1, n1) % 128) / 128
    scale = 1.0 / math.sqrt(NX)
    cos, sin = np.cos(angle) * scale, np.sin(angle) * scale
    real_rows = np.concatenate([cos, -sin], axis=1).reshape(DX, 1, 4, 256)
    imag_rows = np.concatenate([sin, cos], axis=1).reshape(DX, 1, 4, 256)
    weights = np.concatenate([real_rows, imag_rows], axis=1).reshape(256, 256)
    turn = 2.0 * np.pi * np.outer(np.arange(16), n1) / NX
    twiddle = np.stack([np.cos(turn), np.sin(turn)], axis=1).reshape(32, 128)
    return *halves(weights), twiddle.astype(np.float32)


def table_wave():
    wave = 2.0 * np.sin(np.pi * np.arange(NX) / NX)
    return (wave * wave).astype(np.float32).reshape(1, NX)


def dot3(a, b, dims):
    (a_high, a_low), (b_high, b_low) = a, b
    dot = functools.partial(
        lax.dot_general, dimension_numbers=(dims, ((), ())), preferred_element_type=jnp.float32
    )
    return dot(a_high, b_high) + (dot(a_low, b_high) + dot(a_high, b_low))


def pick(codes, table_ref):
    first, second, third = table_ref[0], table_ref[1], table_ref[2]
    return jnp.where(codes == 0, first, jnp.where(codes == 1, second, third))


def pick_row(codes, rows_ref, table):
    first, second, third = (rows_ref[4 * table + m : 4 * table + m + 1, :] for m in range(3))
    return jnp.where(codes == 0, first, jnp.where(codes == 1, second, third))


def lanes(values):
    return lax.broadcasted_iota(jnp.int32, values.shape, values.ndim - 1)


def rows(values):
    return lax.broadcasted_iota(jnp.int32, values.shape, values.ndim - 2)


def next_lane(values):
    moved = pltpu.roll(values, values.shape[-1] - 1, values.ndim - 1)
    return jnp.where(lanes(values) == values.shape[-1] - 1, 0.0, moved)


def last_lane(values):
    moved = pltpu.roll(values, 1, values.ndim - 1)
    return jnp.where(lanes(values) == 0, 0.0, moved)


def next_row(values, edge):
    size = values.shape[0]
    moved = pltpu.roll(values, size - 1, 0)
    tail = moved[size - 8 :]
    tail = jnp.where(rows(tail) == 7, edge, tail)
    return jnp.concatenate([moved[: size - 8], tail], axis=0)


def last_row(values, edge):
    moved = pltpu.roll(values, 1, 0)
    head = jnp.where(rows(moved[:8]) == 0, edge, moved[:8])
    return jnp.concatenate([head, moved[8:]], axis=0)


def next_layer(values):
    size = values.shape[0]
    moved = pltpu.roll(values, size - 1, 0)
    return jnp.where(rows(values) == size - 1, 0.0, moved)


def last_layer(values):
    moved = pltpu.roll(values, 1, 0)
    return jnp.where(rows(values) == 0, 0.0, moved)


def odd(axis):
    return lax.axis_index(axis) % 2 == 1


def low_high(axis, first, second):
    is_odd = odd(axis)
    low = [jnp.where(is_odd, first[c], second[c]) for c in range(first.shape[0])]
    high = [jnp.where(is_odd, second[c], first[c]) for c in range(first.shape[0])]
    return low, high


def edge_rows(
    buoy_in, lame_in, shear_in, piezo_in, stress_in, veloc_in, material_in, second, first, tables,
    stress, veloc, material, buoy, lame, shear, piezo, sems, table_sems,
):
    pairs = [(buoy_in, buoy), (lame_in, lame), (shear_in, shear), (piezo_in, piezo)]
    moves = [pltpu.make_async_copy(*pair, table_sems.at[n]) for n, pair in enumerate(pairs)]
    for n, row in enumerate((0, BX - 1)):
        at = pl.ds(row, 1)
        moves += [
            pltpu.make_async_copy(stress_in.at[:, :, at], stress.at[n], sems.at[n, 0]),
            pltpu.make_async_copy(veloc_in.at[:, :, at], veloc.at[n], sems.at[n, 1]),
            pltpu.make_async_copy(material_in.at[:, at], material.at[n], sems.at[n, 2]),
        ]
    for move in moves:
        move.start()
    for move in moves:
        move.wait()
    sxx, sxy, sxz = (stress[1, c, :, 0, :] for c in (0, 3, 4))
    b = pick(material[1, :, 0, :], buoy)
    ux = veloc[1, 0, :, 0, :] + b * ((sxy - last_lane(sxy)) + (sxz - last_layer(sxz)) - sxx)
    down = [ux, b, sxy, sxz, jnp.zeros_like(b), jnp.zeros_like(b)]
    sxx, syy, szz, sxy, sxz, syz = (stress[0, c, :, 0, :] for c in range(6))
    b = pick(material[0, :, 0, :], buoy)
    uy = veloc[0, 1, :, 0, :] + b * (sxy + (next_lane(syy) - syy) + (syz - last_layer(syz)))
    uz = veloc[0, 2, :, 0, :] + b * (sxz + (syz - last_lane(syz)) + (next_layer(szz) - szz))
    up = [uy, uz, b, sxx, syy, syz]
    is_odd = odd("gx")
    for c in range(6):
        first[c] = jnp.where(is_odd, up[c], down[c])
        second[c] = jnp.where(is_odd, down[c], up[c])
    tables[...] = jnp.zeros_like(tables)
    for n, (_, table) in enumerate(pairs):
        for m in range(3):
            tables[4 * n + m : 4 * n + m + 1, :] = jnp.full((1, BY), table[m])


CHUNK = 2


def copies(pairs, sems):
    made = []
    for k in range(NZ // CHUNK):
        at = pl.ds(k * CHUNK, CHUNK)
        made.append([])
        for n, (source, target) in enumerate(pairs):
            index = (at,) if len(source.shape) == 3 else (slice(None), at)
            made[-1].append(pltpu.make_async_copy(source.at[index], target.at[index], sems.at[k, n]))
    return made


def advance_velocity(tables, stress, veloc, material, new, right_ref, left_ref):
    column = lax.broadcasted_iota(jnp.int32, (BX, BY), 1)
    right = jnp.zeros((BX, BY), jnp.float32)
    left = jnp.zeros((BX, BY), jnp.float32)
    for z in range(NZ):
        sxx, syy, szz, sxy, sxz, syz = (stress[c, z] for c in range(6))
        b = pick_row(material[z], tables, 0)
        dz_sxz = sxz - stress[4, z - 1] if z else sxz
        dz_syz = syz - stress[5, z - 1] if z else syz
        dz_szz = stress[2, z + 1] - szz if z < NZ - 1 else -szz
        ux = veloc[0, z] + b * ((next_row(sxx, 0.0) - sxx) + (sxy - last_lane(sxy)) + dz_sxz)
        uy = veloc[1, z] + b * ((sxy - last_row(sxy, 0.0)) + (next_lane(syy) - syy) + dz_syz)
        uz = veloc[2, z] + b * ((sxz - last_row(sxz, 0.0)) + (syz - last_lane(syz)) + dz_szz)
        new[0, z] = ux
        new[1, z] = uy
        new[2, z] = uz
        for part, value in enumerate((uy, b, sxy, syz)):
            spot = part * NZ + z
            moved = pltpu.roll(value, (spot + 1) % BY, 1)
            right = jnp.where(column == spot, moved, right)
        for part, value in enumerate((ux, uz, b, syy)):
            spot = part * NZ + z
            moved = pltpu.roll(value, spot, 1) if spot else value
            left = jnp.where(column == spot, moved, left)
    right_ref[...] = right
    left_ref[...] = left


def edge_columns(right_ref, left_ref, x_second, x_first, second, first):
    low, high = low_high("gx", x_first, x_second)
    corner = lax.broadcasted_iota(jnp.int32, (NZ, BY), 1)
    layer = lax.broadcasted_iota(jnp.int32, (NZ, BY), 0)
    row = lax.broadcasted_iota(jnp.int32, (BX, BY), 0)
    column = lax.broadcasted_iota(jnp.int32, (BX, BY), 1)

    def line(values, spot, at):
        wide = jnp.broadcast_to(values[:, spot : spot + 1], (NZ, BY))
        return jnp.sum(jnp.where(corner == layer + at, wide, 0.0), axis=0, keepdims=True)

    def shifted(values, by):
        return pltpu.roll(values, (-by * NZ) % BY, 1)

    right, left = right_ref[...], left_ref[...]
    right_b = shifted(right, 1)
    right = right - jnp.where((row == 0) & (column < NZ), right_b * line(low[2], BY - 1, 0), 0.0)
    left_b = jnp.where(column < NZ, shifted(left, 2), shifted(left, 1))
    left = left + jnp.where((row == BX - 1) & (column < NZ), left_b * line(high[3], 0, 0), 0.0)
    left = left - jnp.where(
        (row == 0) & (column >= NZ) & (column < 2 * NZ), left_b * line(low[3], 0, NZ), 0.0
    )
    right_corner = jnp.where(
        corner == 0, pltpu.roll(low[2], 1, 1), jnp.where(corner == 1, pltpu.roll(high[5], 2, 1), 0.0)
    )
    left_corner = jnp.where(corner == 0, high[4], 0.0)
    is_odd = odd("gy")
    first[:BX] = jnp.where(is_odd, left, right)
    first[BX:] = jnp.where(is_odd, left_corner, right_corner)
    second[:BX] = jnp.where(is_odd, right, left)
    second[BX:] = jnp.where(is_odd, right_corner, left_corner)


def advance_stress(
    tables, stress, part, material, x_second, x_first,
    own_right, own_left, y_second, y_first, stress_out, veloc_out, charge,
    new_stress, new_veloc, sems,
):
    leaving = copies([(new_stress, stress_out), (new_veloc, veloc_out)], sems)
    lane = lax.broadcasted_iota(jnp.int32, (BX, BY), 1)
    corner_lane = lane[:NZ]
    row8 = lax.broadcasted_iota(jnp.int32, (8, BY), 0)
    low, high = low_high("gx", x_first, x_second)
    y_odd = odd("gy")
    from_left = jnp.where(y_odd, y_first[...], y_second[...])
    from_right = jnp.where(y_odd, y_second[...], y_first[...])
    west, east = from_left[:BX], from_right[:BX]
    mine_east, mine_west = own_right[...], own_left[...]

    def shifted(values, by):
        return pltpu.roll(values, (-by * NZ) % BY, 1)

    uy_west = west + shifted(west, 1) * shifted(mine_west, 3)
    ux_east = east - shifted(east, 2) * shifted(mine_east, 2)
    uz_east = shifted(east, 1) - shifted(east, 2) * shifted(mine_east, 3)
    west_corner, east_corner = from_left[BX:], from_right[BX:]
    ux_low = low[0] - jnp.where(corner_lane == 0, low[1] * west_corner[:, 0:1], 0.0)
    uy_high = high[0] + jnp.where(corner_lane == BY - 1, high[2] * east_corner[:, 0:1], 0.0)
    uz_high = high[1] - jnp.where(corner_lane == 0, high[2] * west_corner[:, 1:2], 0.0)

    def beside(values, spot):
        return jnp.broadcast_to(values[:, spot : spot + 1], (BX, BY))

    def at_top(values, added):
        head = values[:8] + jnp.where(row8 == 0, added, 0.0)
        return jnp.concatenate([head, values[8:]], axis=0)

    def at_end(values, added):
        tail = values[BX - 8 :] + jnp.where(row8 == 7, added, 0.0)
        return jnp.concatenate([values[: BX - 8], tail], axis=0)

    def close_edges(z):
        b = pick_row(material[z], tables, 0)
        row = slice(z, z + 1)
        head, tail = b[:8], b[BX - 8 :]
        ux = part[0, z] - jnp.where(lane == 0, b * beside(west, 2 * NZ + z), 0.0)
        uy = part[1, z] + jnp.where(lane == BY - 1, b * beside(east, 3 * NZ + z), 0.0)
        uz = part[2, z] - jnp.where(lane == 0, b * beside(west, 3 * NZ + z), 0.0)
        new_veloc[0, z] = at_end(ux, tail * high[3][row])
        new_veloc[1, z] = at_top(uy, -(head * low[2][row]))
        new_veloc[2, z] = at_top(uz, -(head * low[3][row]))

    for step in range(NZ + 1):
        if step < NZ:
            close_edges(step)
        if step == 0:
            continue
        z = step - 1
        sxx, syy, szz, sxy, sxz, syz = (stress[c, z] for c in range(6))
        ux, uy, uz = (new_veloc[c, z] for c in range(3))
        codes = material[z]
        lam, mu, e = (pick_row(codes, tables, table) for table in (1, 2, 3))
        row = slice(z, z + 1)
        ex = ux - last_row(ux, ux_low[row] + low[1][row] * sxx[0:1])
        ey = uy - jnp.where(lane == 0, beside(uy_west, z), pltpu.roll(uy, 1, 1))
        ez = uz - new_veloc[2, z - 1] if z else uz
        lam_div = lam * (ex + ey + ez)
        mu2 = 2.0 * mu
        new_stress[0, z] = sxx + lam_div + mu2 * ex
        new_stress[1, z] = syy + lam_div + mu2 * ey
        new_stress[2, z] = szz + lam_div + mu2 * ez
        b_high = high[2][row]
        dx_uy = next_row(uy, uy_high[row] - b_high * sxy[BX - 1 : BX]) - uy
        dx_uz = next_row(uz, uz_high[row] - b_high * sxz[BX - 1 : BX]) - uz
        last = lane == BY - 1
        dy_ux = jnp.where(last, beside(ux_east, z), pltpu.roll(ux, BY - 1, 1)) - ux
        dy_uz = jnp.where(last, beside(uz_east, z), pltpu.roll(uz, BY - 1, 1)) - uz
        dz_ux = new_veloc[0, z + 1] - ux if z < NZ - 1 else -ux
        dz_uy = new_veloc[1, z + 1] - uy if z < NZ - 1 else -uy
        new_sxz = sxz + mu * (dz_ux + dx_uz)
        new_syz = syz + mu * (dz_uy + dy_uz)
        new_stress[3, z] = sxy + mu * (dy_ux + dx_uy)
        new_stress[4, z] = new_sxz
        new_stress[5, z] = new_syz
        charge[z] = e * (new_sxz + new_syz)
        if z % CHUNK == CHUNK - 1:
            for copy in leaving[z // CHUNK]:
                copy.start()
    for chunk in leaving:
        for copy in chunk:
            copy.wait()


ROOT = math.sqrt(0.5)


def real_dft8(c):
    s = [c[i] + c[i + 4] for i in range(4)]
    d = [c[i] - c[i + 4] for i in range(4)]
    even, odd = s[0] + s[2], s[1] + s[3]
    near, far = ROOT * (d[1] - d[3]), ROOT * (d[1] + d[3])
    re1, re3 = d[0] + near, d[0] - near
    im1, im3 = -(d[2] + far), d[2] - far
    re2, im2 = s[0] - s[2], s[3] - s[1]
    zero = None
    return [
        (even + odd, zero), (re1, im1), (re2, im2), (re3, im3),
        (even - odd, zero), (re3, -im3), (re2, -im2), (re1, -im1),
    ]


def transform_y(charge, w_high, w_low, twiddle, out, real_lines, imag_lines):
    for z in range(2):
        for ihi in range(4):
            at = slice(16 * ihi, 16 * ihi + 16)
            modes = real_dft8([charge[g, z, at, :] for g in range(8)])
            for a, (re, im) in enumerate(modes):
                cos, sin = twiddle[2 * a : 2 * a + 1, :], twiddle[2 * a + 1 : 2 * a + 2, :]
                if a == 0:
                    new_re, new_im = re, jnp.zeros_like(re)
                elif im is None:
                    new_re, new_im = re * cos, -(re * sin)
                else:
                    new_re, new_im = re * cos + im * sin, im * cos - re * sin
                base = (ihi * 2 + a // 4) * 128 + z * 4 + a % 4
                real_lines[pl.ds(base, 16, stride=8), :] = new_re
                imag_lines[pl.ds(base, 16, stride=8), :] = new_im
    weights = (w_high[...], w_low[...])
    for ihi in range(4):
        for ahi in range(2):
            block = slice((ihi * 2 + ahi) * 128, (ihi * 2 + ahi + 1) * 128)
            lines = jnp.concatenate([real_lines[block, :], imag_lines[block, :]], axis=1)
            modes = dot3(weights, split(lines), ((1,), (1,)))
            for part in range(2):
                start = ahi * 8 + part * 4 + ihi
                out[pl.ds(start, 128, stride=16), :] = modes[part * 128 : (part + 1) * 128]


def butterfly4(x):
    (ar, ai), (br, bi) = (
        (x[0][0] + x[2][0], x[0][1] + x[2][1]),
        (x[0][0] - x[2][0], x[0][1] - x[2][1]),
    )
    (cr, ci), (dr, di) = (
        (x[1][0] + x[3][0], x[1][1] + x[3][1]),
        (x[1][0] - x[3][0], x[1][1] - x[3][1]),
    )
    return [(ar + cr, ai + ci), (br + di, bi - dr), (ar - cr, ai - ci), (br - di, bi + dr)]


def turned(value, step):
    re, im = value
    step %= 16
    if step == 0:
        return value
    if step == 4:
        return im, -re
    if step == 2:
        return ROOT * (re + im), ROOT * (im - re)
    if step == 6:
        return ROOT * (im - re), -ROOT * (re + im)
    cos, sin = math.cos(2 * math.pi * step / 16), math.sin(2 * math.pi * step / 16)
    return re * cos + im * sin, im * cos - re * sin


def dft16(x):
    inner = [butterfly4([x[4 * na + nb] for na in range(4)]) for nb in range(4)]
    result = [None] * 16
    for ka in range(4):
        outer = butterfly4([turned(inner[nb][ka], nb * ka) for nb in range(4)])
        for kb in range(4):
            result[ka + 4 * kb] = outer[kb]
    return result


def coupling_scalars(layer_kind, lateral, normal):
    def at(table, kind):
        return jnp.where(kind == 0, table[0], jnp.where(kind == 1, table[1], table[2]))

    el = [at(lateral, layer_kind[z]) for z in range(NZ)]
    en = [at(normal, layer_kind[z]) for z in range(NZ)]
    g = [en[0]] + [0.5 * (en[z - 1] + en[z]) for z in range(1, NZ)] + [en[-1]]
    return el, g


def pivots(layer_kind, lateral, normal, wave_x, inverse, couplings):
    el, g = coupling_scalars(layer_kind, lateral, normal)
    couplings[...] = jnp.zeros_like(couplings)
    for z in range(NZ + 1):
        couplings[z : z + 1, :] = jnp.full((1, 256), g[z])
    first = (lax.axis_index("gx") * DY + lax.axis_index("gy")) * 4
    ky = first + rows(jnp.zeros((8, 128), jnp.float32)) % 4
    wave_y = 2.0 * jnp.sin(math.pi * ky.astype(jnp.float32) / NY)
    wave_y = wave_y * wave_y
    for k in range(NX // 512):
        at = slice(512 * k, 512 * k + 512)
        wave = jnp.concatenate([wave_y] * 4, axis=1) + wave_x[:, at]
        factor = None
        for z in range(NZ):
            pivot = g[z] + g[z + 1] + wave * el[z]
            if z:
                pivot = pivot - g[z] * factor
            inv = 1.0 / pivot
            inverse[z, :, at] = inv
            factor = g[z + 1] * inv


SPAN = 512


def solve(lines, w_high, w_low, twiddle, inverse, couplings, modes_out, rhs, out, sems):
    weights = (w_high[...], w_low[...])
    upper = rows(jnp.zeros((8, 128), jnp.float32)) < 4
    for gy in range(DY):
        block = lines[:, gy].reshape(256, 128)
        modes = dot3(split(block.T), weights, ((1,), (0,)))
        turned_modes = []
        for n2 in range(16):
            re, im = modes[8 * n2 : 8 * n2 + 8, :128], modes[8 * n2 : 8 * n2 + 8, 128:]
            if n2:
                cos, sin = twiddle[2 * n2 : 2 * n2 + 1, :], twiddle[2 * n2 + 1 : 2 * n2 + 2, :]
                re, im = re * cos + im * sin, im * cos - re * sin
            turned_modes.append((re, im))
        for k2, (re, im) in enumerate(dft16(turned_modes)):
            at = slice(128 * k2, 128 * k2 + 128)
            rhs[2 * gy, :, at] = jnp.where(upper, re, pltpu.roll(im, 4, 0))
            rhs[2 * gy + 1, :, at] = jnp.where(upper, pltpu.roll(re, 4, 0), im)
    g = [couplings[z : z + 1, :] for z in range(NZ + 1)]
    leaving = []
    for k in range(NX // 256):
        at = slice(256 * k, 256 * k + 256)
        sums = []
        for z in range(NZ):
            value = rhs[z, :, at]
            if z:
                value = value + g[z] * (sums[-1] * inverse[z - 1, :, at])
            sums.append(value)
        above = None
        for z in range(NZ - 1, -1, -1):
            value = sums[z]
            if above is not None:
                value = value + g[z + 1] * above
            above = value * inverse[z, :, at]
            out[0, z, :, at] = above[:4]
            out[1, z, :, at] = above[4:]
        if (k + 1) * 256 % SPAN == 0:
            done = pl.ds((k + 1) * 256 - SPAN, SPAN)
            leaving.append(
                pltpu.make_async_copy(
                    out.at[:, :, :, done], modes_out.at[:, :, :, done], sems.at[len(leaving)]
                )
            )
            leaving[-1].start()
    for copy in leaving:
        copy.wait()


SMEM = pl.BlockSpec(memory_space=pltpu.SMEM)
VMEM = pl.BlockSpec(memory_space=pltpu.VMEM)
ANY = pl.BlockSpec(memory_space=pl.ANY)


def near(*values):
    return tuple(pltpu.with_memory_space_constraint(value, pltpu.VMEM) for value in values)


def call(body, name, outs, in_specs, args, scratch=(), out_specs=None, flops=1_000_000, keep=()):
    shapes = [
        pltpu.VMEM(shape, jnp.float32) if n in keep else jax.ShapeDtypeStruct(shape, jnp.float32)
        for n, shape in enumerate(outs)
    ]
    moved = sum(4 * math.prod(shape) for shape in outs) + sum(4 * v.size for v in args)
    return pl.pallas_call(
        body,
        name=name,
        out_shape=shapes,
        in_specs=in_specs,
        out_specs=out_specs or [VMEM] * len(outs),
        scratch_shapes=list(scratch),
        compiler_params=pltpu.CompilerParams(vmem_limit_bytes=KEPT_LIMIT),
        cost_estimate=pl.CostEstimate(flops=flops, bytes_accessed=moved, transcendentals=0),
    )(*args)


def field(count, dtype=jnp.float32):
    shape = (NZ, BX, BY)
    return pltpu.VMEM(shape if count == 1 else (count, *shape), dtype)


def swaps(axis, second, first):
    def pairs(start):
        both = [(i, i + 1) for i in range(start, lax.axis_size(axis) - 1, 2)]
        return both + [(b, a) for a, b in both]

    second = lax.ppermute(second, axis, pairs(1))
    return second, lax.ppermute(first, axis, pairs(0))


def per_device(
    stress, velocity, material, layer_kind, buoyancy, lame_first, shear_modulus, piezo, permit_lateral, permit_normal
):
    *x_edges, tables = call(
        edge_rows,
        "edge_rows",
        [(6, NZ, BY)] * 2 + [(16, BY)],
        [ANY] * 7,
        tuple(
            pltpu.with_memory_space_constraint(v, pltpu.HBM)
            for v in (buoyancy, lame_first, shear_modulus, piezo, stress, velocity, material)
        ),
        [
            pltpu.VMEM((2, 6, NZ, 1, BY), jnp.float32),
            pltpu.VMEM((2, 3, NZ, 1, BY), jnp.float32),
            pltpu.VMEM((2, NZ, 1, BY), jnp.int32),
            *[pltpu.SMEM((3,), jnp.float32)] * 4,
            pltpu.SemaphoreType.DMA((2, 3)),
            pltpu.SemaphoreType.DMA((4,)),
        ],
        keep=(0, 1, 2),
    )
    x_edges = near(*swaps("gx", *x_edges))
    stress, velocity, material = near(stress, velocity, material)
    part, own_right, own_left = call(
        advance_velocity,
        "advance_velocity",
        [(3, NZ, BX, BY), (BX, BY), (BX, BY)],
        [VMEM] * 4,
        (tables, stress, velocity, material),
        keep=(0, 1, 2),
    )
    own_right, layer_kind = lax.optimization_barrier((own_right, layer_kind))
    inverse, couplings = call(
        pivots,
        "pivots",
        [(NZ, 8, NX), (24, 256)],
        [SMEM] * 3 + [VMEM],
        (layer_kind, permit_lateral, permit_normal, jnp.asarray(table_wave())),
        keep=(0, 1),
    )
    own_right, inverse = lax.optimization_barrier((own_right, inverse))
    own_right, inverse = near(own_right, inverse)
    y_edges = call(
        edge_columns,
        "edge_columns",
        [(BX + NZ, BY)] * 2,
        [VMEM] * 4,
        (own_right, own_left, *x_edges),
        keep=(0, 1),
    )
    y_edges = near(*swaps("gy", *y_edges))
    stress_next, velocity_next, charge = call(
        advance_stress,
        "advance_stress",
        [(6, NZ, BX, BY), (3, NZ, BX, BY), (NZ, BX, BY)],
        [VMEM] * 10,
        (
            tables, stress, part, material,
            *x_edges, own_right, own_left, *y_edges,
        ),
        [field(6), field(3), pltpu.SemaphoreType.DMA((NZ // CHUNK, 2))],
        [ANY, ANY, VMEM],
        keep=(2,),
    )
    charge = lax.all_to_all(charge, "gy", 0, 0, tiled=True).reshape(DY, 2, BX, BY)
    modes, = call(
        transform_y,
        "transform_y",
        [(NY * 2, 128)],
        [VMEM] * 4,
        (*near(charge), *(jnp.asarray(t) for t in tables_y())),
        [pltpu.VMEM((1024, 128), jnp.float32)] * 2,
        keep=(0,),
    )
    lines = lax.all_to_all(modes.reshape(DX * DY, 8, 128), ("gx", "gy"), 0, 0, tiled=True)
    potential_modes, = call(
        solve,
        "solve",
        [(2, NZ, 4, NX)],
        [VMEM] * 6,
        (*near(lines.reshape(DX, DY, 8, 128)), *(jnp.asarray(t) for t in tables_x()), inverse, couplings),
        [
            pltpu.VMEM((NZ, 8, NX), jnp.float32),
            pltpu.VMEM((2, NZ, 4, NX), jnp.float32),
            pltpu.SemaphoreType.DMA((NX // SPAN,)),
        ],
        [ANY],
    )
    return (stress_next, velocity_next, potential_modes)


def solution(mesh):
    spread = P(None, None, "gx", "gy")
    return jax.shard_map(
        per_device,
        mesh=mesh,
        in_specs=(spread, spread, P(None, "gx", "gy")) + (P(),) * 7,
        out_specs=(spread, spread, P(None, None, ("gx", "gy"), None)),
        check_vma=False,
    )
```

```python
import functools
import math

import jax
import jax.numpy as jnp
import ml_dtypes
import numpy as np
from jax import lax
from jax.experimental import pallas as pl
from jax.experimental.pallas import tpu as pltpu
from jax.sharding import PartitionSpec as P

NZ = 16
NX = 2048
NY = 1024
DX = 32
DY = 8
BX = NX // DX
BY = NY // DY
KEPT_LIMIT = 24 * 1024 * 1024


def halves(values):
    high = values.astype(ml_dtypes.bfloat16)
    low = (values - high.astype(np.float64)).astype(ml_dtypes.bfloat16)
    return high, low


def split(values):
    high = values.astype(jnp.bfloat16)
    low = (values - high.astype(jnp.float32)).astype(jnp.bfloat16)
    return high, low


def tables_y():
    j = np.arange(128)
    a = np.arange(8)
    angle = 2.0 * np.pi * (np.outer(j, j) % 128) / 128
    cos, sin = np.cos(angle) / 32.0, np.sin(angle) / 32.0
    weights = np.block([[cos, sin], [-sin, cos]])
    turn = 2.0 * np.pi * np.outer(a, j) / NY
    twiddle = np.stack([np.cos(turn), np.sin(turn)], axis=1).reshape(16, 128)
    return *halves(weights), twiddle.astype(np.float32)


def tables_x():
    n1 = np.arange(128)
    angle = 2.0 * np.pi * (np.outer(n1, n1) % 128) / 128
    scale = 1.0 / math.sqrt(NX)
    cos, sin = np.cos(angle) * scale, np.sin(angle) * scale
    real_rows = np.concatenate([cos, -sin], axis=1).reshape(DX, 1, 4, 256)
    imag_rows = np.concatenate([sin, cos], axis=1).reshape(DX, 1, 4, 256)
    weights = np.concatenate([real_rows, imag_rows], axis=1).reshape(256, 256)
    turn = 2.0 * np.pi * np.outer(np.arange(16), n1) / NX
    twiddle = np.stack([np.cos(turn), np.sin(turn)], axis=1).reshape(32, 128)
    return *halves(weights), twiddle.astype(np.float32)


def table_wave():
    wave = 2.0 * np.sin(np.pi * np.arange(NX) / NX)
    return (wave * wave).astype(np.float32).reshape(1, NX)


def dot3(a, b, dims):
    (a_high, a_low), (b_high, b_low) = a, b
    dot = functools.partial(
        lax.dot_general, dimension_numbers=(dims, ((), ())), preferred_element_type=jnp.float32
    )
    return dot(a_high, b_high) + (dot(a_low, b_high) + dot(a_high, b_low))


def pick(codes, table_ref):
    first, second, third = table_ref[0], table_ref[1], table_ref[2]
    return jnp.where(codes == 0, first, jnp.where(codes == 1, second, third))


def pick_row(codes, rows_ref, table):
    first, second, third = (rows_ref[4 * table + m : 4 * table + m + 1, :] for m in range(3))
    return jnp.where(codes == 0, first, jnp.where(codes == 1, second, third))


def lanes(values):
    return lax.broadcasted_iota(jnp.int32, values.shape, values.ndim - 1)


def rows(values):
    return lax.broadcasted_iota(jnp.int32, values.shape, values.ndim - 2)


def next_lane(values):
    moved = pltpu.roll(values, values.shape[-1] - 1, values.ndim - 1)
    return jnp.where(lanes(values) == values.shape[-1] - 1, 0.0, moved)


def last_lane(values):
    moved = pltpu.roll(values, 1, values.ndim - 1)
    return jnp.where(lanes(values) == 0, 0.0, moved)


def next_row(values, edge):
    size = values.shape[0]
    moved = pltpu.roll(values, size - 1, 0)
    tail = moved[size - 8 :]
    tail = jnp.where(rows(tail) == 7, edge, tail)
    return jnp.concatenate([moved[: size - 8], tail], axis=0)


def last_row(values, edge):
    moved = pltpu.roll(values, 1, 0)
    head = jnp.where(rows(moved[:8]) == 0, edge, moved[:8])
    return jnp.concatenate([head, moved[8:]], axis=0)


def next_layer(values):
    size = values.shape[0]
    moved = pltpu.roll(values, size - 1, 0)
    return jnp.where(rows(values) == size - 1, 0.0, moved)


def last_layer(values):
    moved = pltpu.roll(values, 1, 0)
    return jnp.where(rows(values) == 0, 0.0, moved)


def odd(axis):
    return lax.axis_index(axis) % 2 == 1


def low_high(axis, first, second):
    is_odd = odd(axis)
    low = [jnp.where(is_odd, first[c], second[c]) for c in range(first.shape[0])]
    high = [jnp.where(is_odd, second[c], first[c]) for c in range(first.shape[0])]
    return low, high


def edge_rows(
    buoy_in, lame_in, shear_in, piezo_in, stress_in, veloc_in, material_in, second, first, tables,
    stress, veloc, material, buoy, lame, shear, piezo, sems, table_sems,
):
    pairs = [(buoy_in, buoy), (lame_in, lame), (shear_in, shear), (piezo_in, piezo)]
    moves = [pltpu.make_async_copy(*pair, table_sems.at[n]) for n, pair in enumerate(pairs)]
    for n, row in enumerate((0, BX - 1)):
        at = pl.ds(row, 1)
        moves += [
            pltpu.make_async_copy(stress_in.at[:, :, at], stress.at[n], sems.at[n, 0]),
            pltpu.make_async_copy(veloc_in.at[:, :, at], veloc.at[n], sems.at[n, 1]),
            pltpu.make_async_copy(material_in.at[:, at], material.at[n], sems.at[n, 2]),
        ]
    for move in moves:
        move.start()
    for move in moves:
        move.wait()
    sxx, sxy, sxz = (stress[1, c, :, 0, :] for c in (0, 3, 4))
    b = pick(material[1, :, 0, :], buoy)
    ux = veloc[1, 0, :, 0, :] + b * ((sxy - last_lane(sxy)) + (sxz - last_layer(sxz)) - sxx)
    down = [ux, b, sxy, sxz, jnp.zeros_like(b), jnp.zeros_like(b)]
    sxx, syy, szz, sxy, sxz, syz = (stress[0, c, :, 0, :] for c in range(6))
    b = pick(material[0, :, 0, :], buoy)
    uy = veloc[0, 1, :, 0, :] + b * (sxy + (next_lane(syy) - syy) + (syz - last_layer(syz)))
    uz = veloc[0, 2, :, 0, :] + b * (sxz + (syz - last_lane(syz)) + (next_layer(szz) - szz))
    up = [uy, uz, b, sxx, syy, syz]
    is_odd = odd("gx")
    for c in range(6):
        first[c] = jnp.where(is_odd, up[c], down[c])
        second[c] = jnp.where(is_odd, down[c], up[c])
    tables[...] = jnp.zeros_like(tables)
    for n, (_, table) in enumerate(pairs):
        for m in range(3):
            tables[4 * n + m : 4 * n + m + 1, :] = jnp.full((1, BY), table[m])


CHUNK = 2


def copies(pairs, sems):
    made = []
    for k in range(NZ // CHUNK):
        at = pl.ds(k * CHUNK, CHUNK)
        made.append([])
        for n, (source, target) in enumerate(pairs):
            index = (at,) if len(source.shape) == 3 else (slice(None), at)
            made[-1].append(pltpu.make_async_copy(source.at[index], target.at[index], sems.at[k, n]))
    return made


def advance_velocity(tables, stress, veloc, material, new, right_ref, left_ref):
    column = lax.broadcasted_iota(jnp.int32, (BX, BY), 1)
    right = jnp.zeros((BX, BY), jnp.float32)
    left = jnp.zeros((BX, BY), jnp.float32)
    for z in range(NZ):
        sxx, syy, szz, sxy, sxz, syz = (stress[c, z] for c in range(6))
        b = pick_row(material[z], tables, 0)
        dz_sxz = sxz - stress[4, z - 1] if z else sxz
        dz_syz = syz - stress[5, z - 1] if z else syz
        dz_szz = stress[2, z + 1] - szz if z < NZ - 1 else -szz
        ux = veloc[0, z] + b * ((next_row(sxx, 0.0) - sxx) + (sxy - last_lane(sxy)) + dz_sxz)
        uy = veloc[1, z] + b * ((sxy - last_row(sxy, 0.0)) + (next_lane(syy) - syy) + dz_syz)
        uz = veloc[2, z] + b * ((sxz - last_row(sxz, 0.0)) + (syz - last_lane(syz)) + dz_szz)
        new[0, z] = ux
        new[1, z] = uy
        new[2, z] = uz
        for part, value in enumerate((uy, b, sxy, syz)):
            spot = part * NZ + z
            moved = pltpu.roll(value, (spot + 1) % BY, 1)
            right = jnp.where(column == spot, moved, right)
        for part, value in enumerate((ux, uz, b, syy)):
            spot = part * NZ + z
            moved = pltpu.roll(value, spot, 1) if spot else value
            left = jnp.where(column == spot, moved, left)
    right_ref[...] = right
    left_ref[...] = left


def edge_columns(right_ref, left_ref, x_second, x_first, second, first):
    low, high = low_high("gx", x_first, x_second)
    corner = lax.broadcasted_iota(jnp.int32, (NZ, BY), 1)
    layer = lax.broadcasted_iota(jnp.int32, (NZ, BY), 0)
    row = lax.broadcasted_iota(jnp.int32, (BX, BY), 0)
    column = lax.broadcasted_iota(jnp.int32, (BX, BY), 1)

    def line(values, spot, at):
        wide = jnp.broadcast_to(values[:, spot : spot + 1], (NZ, BY))
        return jnp.sum(jnp.where(corner == layer + at, wide, 0.0), axis=0, keepdims=True)

    def shifted(values, by):
        return pltpu.roll(values, (-by * NZ) % BY, 1)

    right, left = right_ref[...], left_ref[...]
    right_b = shifted(right, 1)
    right = right - jnp.where((row == 0) & (column < NZ), right_b * line(low[2], BY - 1, 0), 0.0)
    left_b = jnp.where(column < NZ, shifted(left, 2), shifted(left, 1))
    left = left + jnp.where((row == BX - 1) & (column < NZ), left_b * line(high[3], 0, 0), 0.0)
    left = left - jnp.where(
        (row == 0) & (column >= NZ) & (column < 2 * NZ), left_b * line(low[3], 0, NZ), 0.0
    )
    right_corner = jnp.where(
        corner == 0, pltpu.roll(low[2], 1, 1), jnp.where(corner == 1, pltpu.roll(high[5], 2, 1), 0.0)
    )
    left_corner = jnp.where(corner == 0, high[4], 0.0)
    is_odd = odd("gy")
    first[:BX] = jnp.where(is_odd, left, right)
    first[BX:] = jnp.where(is_odd, left_corner, right_corner)
    second[:BX] = jnp.where(is_odd, right, left)
    second[BX:] = jnp.where(is_odd, right_corner, left_corner)


def advance_stress(
    tables, stress, part, material, x_second, x_first,
    own_right, own_left, y_second, y_first, stress_out, new_veloc, charge, new_stress, sems,
):
    leaving = copies([(new_stress, stress_out)], sems)
    lane = lax.broadcasted_iota(jnp.int32, (BX, BY), 1)
    corner_lane = lane[:NZ]
    row8 = lax.broadcasted_iota(jnp.int32, (8, BY), 0)
    low, high = low_high("gx", x_first, x_second)
    y_odd = odd("gy")
    from_left = jnp.where(y_odd, y_first[...], y_second[...])
    from_right = jnp.where(y_odd, y_second[...], y_first[...])
    west, east = from_left[:BX], from_right[:BX]
    mine_east, mine_west = own_right[...], own_left[...]

    def shifted(values, by):
        return pltpu.roll(values, (-by * NZ) % BY, 1)

    uy_west = west + shifted(west, 1) * shifted(mine_west, 3)
    ux_east = east - shifted(east, 2) * shifted(mine_east, 2)
    uz_east = shifted(east, 1) - shifted(east, 2) * shifted(mine_east, 3)
    west_corner, east_corner = from_left[BX:], from_right[BX:]
    ux_low = low[0] - jnp.where(corner_lane == 0, low[1] * west_corner[:, 0:1], 0.0)
    uy_high = high[0] + jnp.where(corner_lane == BY - 1, high[2] * east_corner[:, 0:1], 0.0)
    uz_high = high[1] - jnp.where(corner_lane == 0, high[2] * west_corner[:, 1:2], 0.0)

    def beside(values, spot):
        return jnp.broadcast_to(values[:, spot : spot + 1], (BX, BY))

    def at_top(values, added):
        head = values[:8] + jnp.where(row8 == 0, added, 0.0)
        return jnp.concatenate([head, values[8:]], axis=0)

    def at_end(values, added):
        tail = values[BX - 8 :] + jnp.where(row8 == 7, added, 0.0)
        return jnp.concatenate([values[: BX - 8], tail], axis=0)

    def close_edges(z):
        b = pick_row(material[z], tables, 0)
        row = slice(z, z + 1)
        head, tail = b[:8], b[BX - 8 :]
        ux = part[0, z] - jnp.where(lane == 0, b * beside(west, 2 * NZ + z), 0.0)
        uy = part[1, z] + jnp.where(lane == BY - 1, b * beside(east, 3 * NZ + z), 0.0)
        uz = part[2, z] - jnp.where(lane == 0, b * beside(west, 3 * NZ + z), 0.0)
        new_veloc[0, z] = at_end(ux, tail * high[3][row])
        new_veloc[1, z] = at_top(uy, -(head * low[2][row]))
        new_veloc[2, z] = at_top(uz, -(head * low[3][row]))

    for step in range(NZ + 1):
        if step < NZ:
            close_edges(step)
        if step == 0:
            continue
        z = step - 1
        sxx, syy, szz, sxy, sxz, syz = (stress[c, z] for c in range(6))
        ux, uy, uz = (new_veloc[c, z] for c in range(3))
        codes = material[z]
        lam, mu, e = (pick_row(codes, tables, table) for table in (1, 2, 3))
        row = slice(z, z + 1)
        ex = ux - last_row(ux, ux_low[row] + low[1][row] * sxx[0:1])
        ey = uy - jnp.where(lane == 0, beside(uy_west, z), pltpu.roll(uy, 1, 1))
        ez = uz - new_veloc[2, z - 1] if z else uz
        lam_div = lam * (ex + ey + ez)
        mu2 = 2.0 * mu
        new_stress[0, z] = sxx + lam_div + mu2 * ex
        new_stress[1, z] = syy + lam_div + mu2 * ey
        new_stress[2, z] = szz + lam_div + mu2 * ez
        b_high = high[2][row]
        dx_uy = next_row(uy, uy_high[row] - b_high * sxy[BX - 1 : BX]) - uy
        dx_uz = next_row(uz, uz_high[row] - b_high * sxz[BX - 1 : BX]) - uz
        last = lane == BY - 1
        dy_ux = jnp.where(last, beside(ux_east, z), pltpu.roll(ux, BY - 1, 1)) - ux
        dy_uz = jnp.where(last, beside(uz_east, z), pltpu.roll(uz, BY - 1, 1)) - uz
        dz_ux = new_veloc[0, z + 1] - ux if z < NZ - 1 else -ux
        dz_uy = new_veloc[1, z + 1] - uy if z < NZ - 1 else -uy
        new_sxz = sxz + mu * (dz_ux + dx_uz)
        new_syz = syz + mu * (dz_uy + dy_uz)
        new_stress[3, z] = sxy + mu * (dy_ux + dx_uy)
        new_stress[4, z] = new_sxz
        new_stress[5, z] = new_syz
        charge[z] = e * (new_sxz + new_syz)
        if z % CHUNK == CHUNK - 1:
            for copy in leaving[z // CHUNK]:
                copy.start()
    for chunk in leaving:
        for copy in chunk:
            copy.wait()


ROOT = math.sqrt(0.5)


def real_dft8(c):
    s = [c[i] + c[i + 4] for i in range(4)]
    d = [c[i] - c[i + 4] for i in range(4)]
    even, odd = s[0] + s[2], s[1] + s[3]
    near, far = ROOT * (d[1] - d[3]), ROOT * (d[1] + d[3])
    re1, re3 = d[0] + near, d[0] - near
    im1, im3 = -(d[2] + far), d[2] - far
    re2, im2 = s[0] - s[2], s[3] - s[1]
    zero = None
    return [
        (even + odd, zero), (re1, im1), (re2, im2), (re3, im3),
        (even - odd, zero), (re3, -im3), (re2, -im2), (re1, -im1),
    ]


def transform_y(
    charge, w_high, w_low, twiddle, veloc, out, veloc_out, real_lines, imag_lines, veloc_sem
):
    leaving = pltpu.make_async_copy(veloc, veloc_out, veloc_sem)
    leaving.start()
    for z in range(2):
        for ihi in range(4):
            at = slice(16 * ihi, 16 * ihi + 16)
            modes = real_dft8([charge[g, z, at, :] for g in range(8)])
            for a, (re, im) in enumerate(modes):
                cos, sin = twiddle[2 * a : 2 * a + 1, :], twiddle[2 * a + 1 : 2 * a + 2, :]
                if a == 0:
                    new_re, new_im = re, jnp.zeros_like(re)
                elif im is None:
                    new_re, new_im = re * cos, -(re * sin)
                else:
                    new_re, new_im = re * cos + im * sin, im * cos - re * sin
                base = (ihi * 2 + a // 4) * 128 + z * 4 + a % 4
                real_lines[pl.ds(base, 16, stride=8), :] = new_re
                imag_lines[pl.ds(base, 16, stride=8), :] = new_im
    weights = (w_high[...], w_low[...])
    for ihi in range(4):
        for ahi in range(2):
            block = slice((ihi * 2 + ahi) * 128, (ihi * 2 + ahi + 1) * 128)
            lines = jnp.concatenate([real_lines[block, :], imag_lines[block, :]], axis=1)
            modes = dot3(weights, split(lines), ((1,), (1,)))
            for part in range(2):
                start = ahi * 8 + part * 4 + ihi
                out[pl.ds(start, 128, stride=16), :] = modes[part * 128 : (part + 1) * 128]
    leaving.wait()


def butterfly4(x):
    (ar, ai), (br, bi) = (
        (x[0][0] + x[2][0], x[0][1] + x[2][1]),
        (x[0][0] - x[2][0], x[0][1] - x[2][1]),
    )
    (cr, ci), (dr, di) = (
        (x[1][0] + x[3][0], x[1][1] + x[3][1]),
        (x[1][0] - x[3][0], x[1][1] - x[3][1]),
    )
    return [(ar + cr, ai + ci), (br + di, bi - dr), (ar - cr, ai - ci), (br - di, bi + dr)]


def turned(value, step):
    re, im = value
    step %= 16
    if step == 0:
        return value
    if step == 4:
        return im, -re
    if step == 2:
        return ROOT * (re + im), ROOT * (im - re)
    if step == 6:
        return ROOT * (im - re), -ROOT * (re + im)
    cos, sin = math.cos(2 * math.pi * step / 16), math.sin(2 * math.pi * step / 16)
    return re * cos + im * sin, im * cos - re * sin


def dft16(x):
    inner = [butterfly4([x[4 * na + nb] for na in range(4)]) for nb in range(4)]
    result = [None] * 16
    for ka in range(4):
        outer = butterfly4([turned(inner[nb][ka], nb * ka) for nb in range(4)])
        for kb in range(4):
            result[ka + 4 * kb] = outer[kb]
    return result


def coupling_scalars(layer_kind, lateral, normal):
    def at(table, kind):
        return jnp.where(kind == 0, table[0], jnp.where(kind == 1, table[1], table[2]))

    el = [at(lateral, layer_kind[z]) for z in range(NZ)]
    en = [at(normal, layer_kind[z]) for z in range(NZ)]
    g = [en[0]] + [0.5 * (en[z - 1] + en[z]) for z in range(1, NZ)] + [en[-1]]
    return el, g


def pivots(layer_kind, lateral, normal, wave_x, inverse, couplings):
    el, g = coupling_scalars(layer_kind, lateral, normal)
    couplings[...] = jnp.zeros_like(couplings)
    for z in range(NZ + 1):
        couplings[z : z + 1, :] = jnp.full((1, 256), g[z])
    first = (lax.axis_index("gx") * DY + lax.axis_index("gy")) * 4
    ky = first + rows(jnp.zeros((8, 128), jnp.float32)) % 4
    wave_y = 2.0 * jnp.sin(math.pi * ky.astype(jnp.float32) / NY)
    wave_y = wave_y * wave_y
    for k in range(NX // 512):
        at = slice(512 * k, 512 * k + 512)
        wave = jnp.concatenate([wave_y] * 4, axis=1) + wave_x[:, at]
        factor = None
        for z in range(NZ):
            pivot = g[z] + g[z + 1] + wave * el[z]
            if z:
                pivot = pivot - g[z] * factor
            inv = 1.0 / pivot
            inverse[z, :, at] = inv
            factor = g[z + 1] * inv


SPAN = 512


def solve(lines, w_high, w_low, twiddle, inverse, couplings, modes_out, rhs, out, sems):
    weights = (w_high[...], w_low[...])
    upper = rows(jnp.zeros((8, 128), jnp.float32)) < 4
    for gy in range(DY):
        block = lines[:, gy].reshape(256, 128)
        modes = dot3(split(block.T), weights, ((1,), (0,)))
        turned_modes = []
        for n2 in range(16):
            re, im = modes[8 * n2 : 8 * n2 + 8, :128], modes[8 * n2 : 8 * n2 + 8, 128:]
            if n2:
                cos, sin = twiddle[2 * n2 : 2 * n2 + 1, :], twiddle[2 * n2 + 1 : 2 * n2 + 2, :]
                re, im = re * cos + im * sin, im * cos - re * sin
            turned_modes.append((re, im))
        for k2, (re, im) in enumerate(dft16(turned_modes)):
            at = slice(128 * k2, 128 * k2 + 128)
            rhs[2 * gy, :, at] = jnp.where(upper, re, pltpu.roll(im, 4, 0))
            rhs[2 * gy + 1, :, at] = jnp.where(upper, pltpu.roll(re, 4, 0), im)
    g = [couplings[z : z + 1, :] for z in range(NZ + 1)]
    leaving = []
    for k in range(NX // 256):
        at = slice(256 * k, 256 * k + 256)
        sums = []
        for z in range(NZ):
            value = rhs[z, :, at]
            if z:
                value = value + g[z] * (sums[-1] * inverse[z - 1, :, at])
            sums.append(value)
        above = None
        for z in range(NZ - 1, -1, -1):
            value = sums[z]
            if above is not None:
                value = value + g[z + 1] * above
            above = value * inverse[z, :, at]
            out[0, z, :, at] = above[:4]
            out[1, z, :, at] = above[4:]
        if (k + 1) * 256 % SPAN == 0:
            done = pl.ds((k + 1) * 256 - SPAN, SPAN)
            leaving.append(
                pltpu.make_async_copy(
                    out.at[:, :, :, done], modes_out.at[:, :, :, done], sems.at[len(leaving)]
                )
            )
            leaving[-1].start()
    for copy in leaving:
        copy.wait()


SMEM = pl.BlockSpec(memory_space=pltpu.SMEM)
VMEM = pl.BlockSpec(memory_space=pltpu.VMEM)
ANY = pl.BlockSpec(memory_space=pl.ANY)


def near(*values):
    return tuple(pltpu.with_memory_space_constraint(value, pltpu.VMEM) for value in values)


def call(body, name, outs, in_specs, args, scratch=(), out_specs=None, flops=1_000_000, keep=()):
    shapes = [
        pltpu.VMEM(shape, jnp.float32) if n in keep else jax.ShapeDtypeStruct(shape, jnp.float32)
        for n, shape in enumerate(outs)
    ]
    moved = sum(4 * math.prod(shape) for shape in outs) + sum(4 * v.size for v in args)
    return pl.pallas_call(
        body,
        name=name,
        out_shape=shapes,
        in_specs=in_specs,
        out_specs=out_specs or [VMEM] * len(outs),
        scratch_shapes=list(scratch),
        compiler_params=pltpu.CompilerParams(vmem_limit_bytes=KEPT_LIMIT),
        cost_estimate=pl.CostEstimate(flops=flops, bytes_accessed=moved, transcendentals=0),
    )(*args)


def field(count, dtype=jnp.float32):
    shape = (NZ, BX, BY)
    return pltpu.VMEM(shape if count == 1 else (count, *shape), dtype)


def swaps(axis, second, first):
    def pairs(start):
        both = [(i, i + 1) for i in range(start, lax.axis_size(axis) - 1, 2)]
        return both + [(b, a) for a, b in both]

    second = lax.ppermute(second, axis, pairs(1))
    return second, lax.ppermute(first, axis, pairs(0))


def per_device(
    stress, velocity, material, layer_kind, buoyancy, lame_first, shear_modulus, piezo, permit_lateral, permit_normal
):
    *x_edges, tables = call(
        edge_rows,
        "edge_rows",
        [(6, NZ, BY)] * 2 + [(16, BY)],
        [ANY] * 7,
        tuple(
            pltpu.with_memory_space_constraint(v, pltpu.HBM)
            for v in (buoyancy, lame_first, shear_modulus, piezo, stress, velocity, material)
        ),
        [
            pltpu.VMEM((2, 6, NZ, 1, BY), jnp.float32),
            pltpu.VMEM((2, 3, NZ, 1, BY), jnp.float32),
            pltpu.VMEM((2, NZ, 1, BY), jnp.int32),
            *[pltpu.SMEM((3,), jnp.float32)] * 4,
            pltpu.SemaphoreType.DMA((2, 3)),
            pltpu.SemaphoreType.DMA((4,)),
        ],
        keep=(0, 1, 2),
    )
    x_edges = near(*swaps("gx", *x_edges))
    stress, velocity, material = near(stress, velocity, material)
    part, own_right, own_left = call(
        advance_velocity,
        "advance_velocity",
        [(3, NZ, BX, BY), (BX, BY), (BX, BY)],
        [VMEM] * 4,
        (tables, stress, velocity, material),
        keep=(0, 1, 2),
    )
    y_edges = call(
        edge_columns,
        "edge_columns",
        [(BX + NZ, BY)] * 2,
        [VMEM] * 4,
        (own_right, own_left, *x_edges),
        keep=(0, 1),
    )
    to_swap, layer_kind = lax.optimization_barrier((tuple(y_edges), layer_kind))
    inverse, couplings = call(
        pivots,
        "pivots",
        [(NZ, 8, NX), (24, 256)],
        [SMEM] * 3 + [VMEM],
        (layer_kind, permit_lateral, permit_normal, jnp.asarray(table_wave())),
        keep=(0, 1),
    )
    y_edges = near(*swaps("gy", *near(*to_swap)))
    own_right, inverse = lax.optimization_barrier((own_right, inverse))
    own_right, inverse = near(own_right, inverse)
    stress_next, closed, charge = call(
        advance_stress,
        "advance_stress",
        [(6, NZ, BX, BY), (3, NZ, BX, BY), (NZ, BX, BY)],
        [VMEM] * 10,
        (
            tables, stress, part, material,
            *x_edges, own_right, own_left, *y_edges,
        ),
        [field(6), pltpu.SemaphoreType.DMA((NZ // CHUNK, 1))],
        [ANY, VMEM, VMEM],
        keep=(1, 2),
    )
    charge = lax.all_to_all(charge, "gy", 0, 0, tiled=True).reshape(DY, 2, BX, BY)
    modes, velocity_next = call(
        transform_y,
        "transform_y",
        [(NY * 2, 128), (3, NZ, BX, BY)],
        [VMEM] * 5,
        (*near(charge), *(jnp.asarray(t) for t in tables_y()), closed),
        [*[pltpu.VMEM((1024, 128), jnp.float32)] * 2, pltpu.SemaphoreType.DMA],
        [VMEM, ANY],
        keep=(0,),
    )
    lines = lax.all_to_all(modes.reshape(DX * DY, 8, 128), ("gx", "gy"), 0, 0, tiled=True)
    potential_modes, = call(
        solve,
        "solve",
        [(2, NZ, 4, NX)],
        [VMEM] * 6,
        (*near(lines.reshape(DX, DY, 8, 128)), *(jnp.asarray(t) for t in tables_x()), inverse, couplings),
        [
            pltpu.VMEM((NZ, 8, NX), jnp.float32),
            pltpu.VMEM((2, NZ, 4, NX), jnp.float32),
            pltpu.SemaphoreType.DMA((NX // SPAN,)),
        ],
        [ANY],
    )
    return (stress_next, velocity_next, potential_modes)


def solution(mesh):
    spread = P(None, None, "gx", "gy")
    return jax.shard_map(
        per_device,
        mesh=mesh,
        in_specs=(spread, spread, P(None, "gx", "gy")) + (P(),) * 7,
        out_specs=(spread, spread, P(None, None, ("gx", "gy"), None)),
        check_vma=False,
    )
```
